256 devices in a mesh: lat: 8 (over z), lon: 16 (over x, y), mem: 2 (over core).
Axes of the slice: x: 4, y: 4, z: 8, core: 2. Of those that a mesh axis runs over, the one named last changes fastest.
Arguments:
- measured_inputs: bfloat16 [4096, 128, 256], P(('lat', 'lon', 'mem')), may hold values from -6 to 6
- target_sector: int32 [4096], P(('lat', 'lon', 'mem')), may hold values from 0 to 15, as said below
- hidden_member_fields: bfloat16 [2, 64, 128, 768], P('mem', 'lat', 'lon'), may hold values from -6 to 6
- analysis_adjoint: bfloat16 [2, 64, 128, 768], P('mem', 'lat', 'lon'), may hold values from -0.29882812 to 0.29882812
- inner_perceptron_coeffs: bfloat16 [256, 256], replicated, may hold values from -0.375 to 0.375
- outer_perceptron_coeffs: bfloat16 [256, 768], replicated, may hold values from -0.375 to 0.375
- probe_projector: bfloat16 [768, 768], replicated, may hold values from -0.21875 to 0.21875
- logit_sharpness: float32 [12], replicated, may hold values from 0.5 to 2.5
- adjacent_channel_coeffs: float32 [8, 768], replicated, may hold values from -0.7 to 0.7
Outputs:
- analysis: bfloat16 [2, 64, 128, 768], P('mem', 'lat', 'lon')
- in_weight_grad: float32 [256, 256], replicated
- out_weight_grad: float32 [256, 768], replicated
The draws below stay inside these ranges and needn't reach their ends.
Inputs may be any that keep to these rules, and one draw needn't show every extreme that they name: `target_sector`: of the 16 blocks of one device at most 2 have one destination, and one destination has exactly 2; in every band and member one sector receives exactly 2 blocks from every device of the band, 32 in all, and no sector receives more.
All inputs are finite; a program needn't handle non-finite values.
Results may differ from the reference program's by a relative error of at most 0.012.
The reference program's roundings to bfloat16 on the way count: a program that leaves them out, or rounds other values in their place, can miss the bound.
Values may be sent and summed in bfloat16 or wider, within the bound.
No kernel may reach another device: no remote copies, remote signals or barrier semaphores. Data moves between devices by JAX's collectives and lax.ppermute only.
A program may use at most 192 MiB of HBM per device.

```python
import math
import jax
import jax.numpy as jnp
from jax import lax

DO = 256
HID = 256
D = 768
HEADS = 12
CHANNELS_PER_ATT = 64
BT = 128
CLAT = 8
CLON = 8
NB_DEV = 16
CAP = 2
TILE_CAP = 32
OBS_BLOCKS = 4096
MEMBERS = 2
LATS = 64
LONS = 128
N_LAT = 8
N_LON = 16
N_MEM = 2


def shuffle_row(row_key, sector_row):
    return jax.random.permutation(row_key, sector_row)


def draw_target_sector(key, part):
    device_count = N_LAT * N_LON * N_MEM
    slot_count = N_LON * CAP
    first_key, second_key, third_key = jax.random.split(key, 3)
    hot_sector = jax.random.randint(first_key, (N_LAT, 1, N_MEM), 0, N_LON)
    hot_sector = jnp.broadcast_to(hot_sector, (N_LAT, N_LON, N_MEM)).reshape(device_count)
    slot_sector = jnp.arange(slot_count, dtype=jnp.int32) // CAP
    noise = jax.random.randint(second_key, (device_count, slot_count), 0, 1 << 20)
    priority = noise * slot_count + jnp.arange(slot_count, dtype=jnp.int32)[None, :]
    priority = jnp.where(slot_sector[None, :] == hot_sector[:, None], priority + (1 << 29), priority)
    unused, picked = lax.top_k(priority, NB_DEV)
    sectors = (picked // CAP).astype(jnp.int32)
    row_keys = jax.random.split(third_key, device_count)
    shuffled = jax.vmap(shuffle_row)(row_keys, sectors)
    return shuffled.reshape(device_count * NB_DEV).astype(jnp.int32)


def draw_logit_sharpness(key, part):
    first_key = jax.random.fold_in(key, 0)
    base_scale = jnp.exp(jax.random.uniform(first_key, (HEADS,), jnp.float32, jnp.log(0.5), jnp.log(2.5)))
    return base_scale.astype(jnp.float32)


def block_scale(own_key, shape, shards, low, top_value):
    loudness, own = 1.0, jax.random.fold_in(own_key, 6)
    for axis_at, parts in shards:
        draws = jnp.exp(jax.random.uniform(jax.random.fold_in(own, axis_at), (parts,), jnp.float32, low / len(shards), top_value / len(shards)))
        loudness = loudness * jnp.repeat(draws, shape[axis_at] // parts).reshape([-1 if axis == axis_at else 1 for axis in range(len(shape))])
    return loudness


def centred(key, shape, scale, reach, cuts=(), held_as=jnp.bfloat16):
    level = block_scale(key, shape, cuts, -0.22, 0.18) if cuts else 1.0
    drawn = jax.random.normal(key, shape, jnp.float32) * scale * level
    return jnp.minimum(jnp.maximum(drawn, -reach), reach).astype(held_as)


def setup_inputs(seed: int = 0) -> dict:
    key_list = jax.random.split(jax.random.key(seed), 10)
    measured_inputs = centred(key_list[0], (OBS_BLOCKS, BT, DO), 1.0, 6.0, ((0, 256),))
    target_sector = draw_target_sector(jax.random.fold_in(key_list[9], 71), 0)
    hidden_member_fields = centred(key_list[2], (MEMBERS, LATS, LONS, D), 1.0, 6.0, ((0, 2), (1, 8), (2, 16)))
    analysis_adjoint = centred(key_list[3], (MEMBERS, LATS, LONS, D), 0.05, 0.29882812, ((0, 2), (1, 8), (2, 16)))
    inner_perceptron_coeffs = centred(key_list[4], (DO, HID), DO ** -0.5, 0.375)
    outer_perceptron_coeffs = centred(key_list[5], (HID, D), HID ** -0.5, 0.375)
    probe_projector = centred(key_list[6], (D, D), D ** -0.5, 0.21875)
    logit_sharpness = draw_logit_sharpness(jax.random.fold_in(key_list[9], 71), 0)
    adjacent_channel_coeffs = jnp.clip(jax.random.uniform(key_list[8], (8, D), jnp.float32, -0.7, 0.7), -0.7, 0.7)
    return dict(measured_inputs=measured_inputs, target_sector=target_sector, hidden_member_fields=hidden_member_fields, analysis_adjoint=analysis_adjoint, inner_perceptron_coeffs=inner_perceptron_coeffs, outer_perceptron_coeffs=outer_perceptron_coeffs, probe_projector=probe_projector, logit_sharpness=logit_sharpness, adjacent_channel_coeffs=adjacent_channel_coeffs)


NEIGHBOURS = ((-1, -1), (-1, 0), (-1, 1), (0, -1), (0, 1), (1, -1), (1, 0), (1, 1))

def rounded(values):
    return lax.optimization_barrier(values.astype(jnp.bfloat16))

def silu_slope(pre_act):
    sigmoid_val = jax.nn.sigmoid(pre_act)
    return sigmoid_val * (1.0 + pre_act * (1.0 - sigmoid_val))

def neighbour_mix(field, adjacent_channel_coeffs, direction):
    values = field.astype(jnp.float32)
    n_rows = values.shape[1]
    n_cols = values.shape[2]
    padded = jnp.pad(values, ((0, 0), (1, 1), (0, 0), (0, 0)))
    padded = jnp.concatenate([padded[:, :, -1:], padded, padded[:, :, :1]], axis=2)
    total = values
    for offset_idx, (row_step, col_step) in enumerate(NEIGHBOURS):
        row_start = 1 + direction * row_step
        col_start = 1 + direction * col_step
        total = total + adjacent_channel_coeffs[offset_idx] * padded[:, row_start:row_start + n_rows, col_start:col_start + n_cols]
    return total

def mutual_attention_apply(probe_projection, grid_point_entries, lookup_projection_entries, genuine_entry_indicator, logit_sharpness):
    n_cells = grid_point_entries.shape[0]
    n_tokens = lookup_projection_entries.shape[0]
    query_heads = probe_projection.reshape(n_cells, HEADS, CHANNELS_PER_ATT).astype(jnp.float32)
    key_heads = lookup_projection_entries.reshape(n_tokens, HEADS, CHANNELS_PER_ATT).astype(jnp.float32)
    latent_heads = grid_point_entries.reshape(n_cells, HEADS, CHANNELS_PER_ATT).astype(jnp.float32)
    normaliser_entries = logit_sharpness / math.sqrt(CHANNELS_PER_ATT)
    scores = jnp.einsum('qhd,khd->hqk', query_heads, key_heads) * normaliser_entries[:, None, None]
    scores = jnp.where(genuine_entry_indicator[None, None, :], scores, -jnp.inf)
    self_score = jnp.einsum('qhd,qhd->hq', query_heads, latent_heads) * normaliser_entries[:, None]
    row_max = jnp.maximum(lax.optimization_barrier(jnp.max(scores, axis=2)), self_score)
    exp_terms = jnp.exp(scores - row_max[:, :, None])
    self_exp = jnp.exp(self_score - row_max)
    denominator = lax.optimization_barrier(jnp.sum(exp_terms, axis=2)) + self_exp
    probs = exp_terms / denominator[:, :, None]
    self_prob = self_exp / denominator
    weights = rounded(probs)
    self_weight = rounded(self_prob)
    update = jnp.einsum('hqk,khd->qhd', weights.astype(jnp.float32), key_heads)
    update = update + jnp.transpose(self_weight.astype(jnp.float32))[:, :, None] * latent_heads
    revised_analysis = rounded(grid_point_entries.astype(jnp.float32) + update.reshape(n_cells, HEADS * CHANNELS_PER_ATT))
    return (revised_analysis, (probs, self_prob, weights))

def mutual_attention_adjoint(probe_projection, grid_point_entries, lookup_projection_entries, retained_intermediates, hidden_field_adjoint, logit_sharpness):
    probs, self_prob, weights = retained_intermediates
    n_cells = grid_point_entries.shape[0]
    n_tokens = lookup_projection_entries.shape[0]
    query_heads = probe_projection.reshape(n_cells, HEADS, CHANNELS_PER_ATT).astype(jnp.float32)
    key_heads = lookup_projection_entries.reshape(n_tokens, HEADS, CHANNELS_PER_ATT).astype(jnp.float32)
    latent_heads = grid_point_entries.reshape(n_cells, HEADS, CHANNELS_PER_ATT).astype(jnp.float32)
    grad_heads = hidden_field_adjoint.reshape(n_cells, HEADS, CHANNELS_PER_ATT).astype(jnp.float32)
    normaliser_entries = logit_sharpness / math.sqrt(CHANNELS_PER_ATT)
    weight_grad = jnp.einsum('qhd,khd->hqk', grad_heads, key_heads)
    self_grad = jnp.einsum('qhd,qhd->hq', grad_heads, latent_heads)
    row_total = lax.optimization_barrier(jnp.sum(probs * weight_grad, axis=2)) + self_prob * self_grad
    logit_grad = rounded(probs * (weight_grad - row_total[:, :, None]) * normaliser_entries[:, None, None])
    measured_embedding_adjoint = jnp.einsum('hqk,qhd->khd', weights.astype(jnp.float32), grad_heads)
    measured_embedding_adjoint = measured_embedding_adjoint + jnp.einsum('hqk,qhd->khd', logit_grad.astype(jnp.float32), query_heads)
    return rounded(measured_embedding_adjoint.reshape(n_tokens, HEADS * CHANNELS_PER_ATT))

def reference(measured_inputs, target_sector, hidden_member_fields, analysis_adjoint, inner_perceptron_coeffs, outer_perceptron_coeffs, probe_projector, logit_sharpness, adjacent_channel_coeffs):
    n_cells = CLAT * CLON
    state_grad_grid = rounded(neighbour_mix(analysis_adjoint, adjacent_channel_coeffs, -1))
    blocks = measured_inputs.reshape(N_LAT, N_LON, N_MEM, NB_DEV, BT, DO).transpose(2, 0, 1, 3, 4, 5)
    blocks = blocks.reshape(N_MEM * N_LAT, N_LON * NB_DEV, BT, DO)
    targets = target_sector.reshape(N_LAT, N_LON, N_MEM, NB_DEV).transpose(2, 0, 1, 3)
    targets = targets.reshape(N_MEM * N_LAT, N_LON * NB_DEV)

    def to_tiles(grid):
        tiles = grid.reshape(N_MEM, N_LAT, CLAT, N_LON, CLON, D).transpose(0, 1, 3, 2, 4, 5)
        return tiles.reshape(N_MEM * N_LAT, N_LON, n_cells, D)
    latent_tiles = to_tiles(hidden_member_fields)
    grad_tiles = to_tiles(state_grad_grid)
    slot_ids = jnp.arange(TILE_CAP * BT, dtype=jnp.int32) // BT
    sector_ids = jnp.arange(N_LON, dtype=jnp.int32)

    def one_band(band_args):
        band_blocks, band_targets, band_latent, band_grad = band_args
        order = jnp.argsort(band_targets, stable=True).astype(jnp.int32)
        sorted_blocks = jnp.concatenate([band_blocks[order], jnp.zeros((TILE_CAP, BT, DO), band_blocks.dtype)], axis=0)
        all_tokens = sorted_blocks.reshape(-1, DO)
        pre_act = jnp.dot(all_tokens, inner_perceptron_coeffs, preferred_element_type=jnp.float32)
        hidden_act = rounded(jax.nn.silu(pre_act))
        obs_feat = rounded(jnp.dot(hidden_act, outer_perceptron_coeffs, preferred_element_type=jnp.float32))
        counts = lax.optimization_barrier(jnp.sum((band_targets[None, :] == sector_ids[:, None]).astype(jnp.int32), axis=1))
        starts = (jnp.cumsum(counts) - counts).astype(jnp.int32)

        def one_tile(carry, tile_args):
            start, count, patchwise_hidden, patchwise_adjoint = tile_args
            token_start = (start * BT).astype(jnp.int32)
            lookup_projection_entries = lax.dynamic_slice_in_dim(obs_feat, token_start, TILE_CAP * BT, 0)
            genuine_entry_indicator = slot_ids < count
            probe_projection = rounded(jnp.dot(patchwise_hidden, probe_projector, preferred_element_type=jnp.float32))
            revised_analysis, retained_intermediates = mutual_attention_apply(probe_projection, patchwise_hidden, lookup_projection_entries, genuine_entry_indicator, logit_sharpness)
            measured_embedding_adjoint = mutual_attention_adjoint(probe_projection, patchwise_hidden, lookup_projection_entries, retained_intermediates, patchwise_adjoint, logit_sharpness)
            current = lax.dynamic_slice_in_dim(carry, token_start, TILE_CAP * BT, 0)
            carry = lax.dynamic_update_slice_in_dim(carry, current + measured_embedding_adjoint, token_start, 0)
            return (carry, revised_analysis)
        start_grad = jnp.zeros(((N_LON * NB_DEV + TILE_CAP) * BT, D), jnp.bfloat16)
        feature_all, states = lax.scan(one_tile, start_grad, (starts, counts, band_latent, band_grad))
        hidden_grad = rounded(jnp.dot(feature_all, outer_perceptron_coeffs.T, preferred_element_type=jnp.float32) * silu_slope(pre_act))
        out_grad = jnp.dot(hidden_act.T, feature_all, preferred_element_type=jnp.float32)
        in_grad = jnp.dot(all_tokens.T, hidden_grad, preferred_element_type=jnp.float32)
        return (states, in_grad, out_grad)
    states, in_parts, out_parts = lax.map(one_band, (blocks, targets, latent_tiles, grad_tiles))
    state_grid = states.reshape(N_MEM, N_LAT, N_LON, CLAT, CLON, D).transpose(0, 1, 3, 2, 4, 5)
    state_grid = state_grid.reshape(N_MEM, LATS, LONS, D)
    analysis = rounded(neighbour_mix(state_grid, adjacent_channel_coeffs, 1))
    return (analysis, lax.optimization_barrier(jnp.sum(in_parts, axis=0)), lax.optimization_barrier(jnp.sum(out_parts, axis=0)))
```

```python
import math

import jax
import jax.numpy as jnp
from jax import lax
from jax.experimental import pallas as pl
from jax.experimental.pallas import tpu as pltpu
from jax.sharding import PartitionSpec as P

HEADS = 12
CHANNELS_PER_ATT = 64
GROUPS = 3
LANES = 256
CHUNK_BLOCKS = 4
MARK = 512.0


NEIGHBOURS = ((-1, -1), (-1, 0), (-1, 1), (0, -1), (0, 1), (1, -1), (1, 0), (1, 1))


def extended(block, sides, width):
    for axis, dim in sides:
        count = lax.axis_size(axis)
        forward = [(i, i + 1) for i in range(count - 1)]
        forward.append((count - 1, 0))
        backward = [(target, source) for source, target in forward]
        low = lax.ppermute(
            lax.slice_in_dim(block, block.shape[dim] - width, None, axis=dim), axis, forward
        )
        high = lax.ppermute(lax.slice_in_dim(block, 0, width, axis=dim), axis, backward)
        block = jnp.concatenate([low, block, high], axis=dim)
    return block


def mix_local(padded, keep_rows, adjacent_channel_coeffs, direction):
    values = padded.astype(jnp.float32) * keep_rows[:, None, None]
    n_rows = padded.shape[0] - 2
    n_cols = padded.shape[1] - 2
    total = values[1 : 1 + n_rows, 1 : 1 + n_cols]
    for offset_idx, (row_step, col_step) in enumerate(NEIGHBOURS):
        row_start = 1 + direction * row_step
        col_start = 1 + direction * col_step
        total = (
            total
            + adjacent_channel_coeffs[offset_idx]
            * values[row_start : row_start + n_rows, col_start : col_start + n_cols]
        )
    return total


def pack_kernel(target_ref, blocks_ref, send_ref, count_ref, mark_ref, sem):
    n_blocks = blocks_ref.shape[0]
    n_dest = send_ref.shape[0]
    cap = send_ref.shape[1]
    mark_ref[...] = jnp.full(mark_ref.shape, MARK, mark_ref.dtype)
    for d in range(n_dest):
        count_ref[d] = 0

    def copy_of(b, dest, slot):
        return pltpu.make_async_copy(blocks_ref.at[b], send_ref.at[dest, slot], sem.at[b])

    for b in range(n_blocks):
        dest = target_ref[b]
        slot = count_ref[dest]
        count_ref[dest] = slot + 1
        copy_of(b, dest, slot).start()

    def mark_of(d, slot):
        return pltpu.make_async_copy(
            mark_ref, send_ref.at[d, slot, pl.ds(0, mark_ref.shape[0])], sem.at[n_blocks + d * cap + slot]
        )

    for d in range(n_dest):
        for slot in range(cap):

            @pl.when(count_ref[d] <= slot)
            def _():
                mark_of(d, slot).start()

    for b in range(n_blocks):
        copy_of(b, 0, 0).wait()
    for d in range(n_dest):
        for slot in range(cap):

            @pl.when(count_ref[d] <= slot)
            def _():
                mark_of(d, slot).wait()


def pack_blocks(target_sector, blocks, n_dest, cap):
    n_blocks, block_len, width = blocks.shape
    return pl.pallas_call(
        pack_kernel,
        out_shape=jax.ShapeDtypeStruct((n_dest, cap, block_len, width), blocks.dtype),
        in_specs=[
            pl.BlockSpec(memory_space=pltpu.SMEM),
            pl.BlockSpec(memory_space=pl.ANY),
        ],
        out_specs=pl.BlockSpec(memory_space=pl.ANY),
        scratch_shapes=[
            pltpu.SMEM((n_dest,), jnp.int32),
            pltpu.VMEM((16, width), blocks.dtype),
            pltpu.SemaphoreType.DMA((n_blocks + n_dest * cap,)),
        ],
        name="pack_blocks",
    )(target_sector, blocks)


def block_mask():
    rows = lax.broadcasted_iota(jnp.int32, (LANES, LANES), 0) // CHANNELS_PER_ATT
    cols = lax.broadcasted_iota(jnp.int32, (LANES, LANES), 1) // CHANNELS_PER_ATT
    return rows == cols


def spread(values, group, mask):
    part = values[:, group * LANES : (group + 1) * LANES].astype(jnp.float32)
    return jnp.where(mask, jnp.concatenate([part] * (LANES // CHANNELS_PER_ATT), axis=0), 0.0)


def cells_kernel(cells_ref, grad_ref, probe_ref, outer_ref, qt_ref, gt_ref, xt_ref, gq_ref, self_ref, ot_ref):
    mask = block_mask()
    query = jnp.dot(cells_ref[...], probe_ref[...], preferred_element_type=jnp.float32)
    query = query.astype(jnp.bfloat16).astype(jnp.float32)
    cells = cells_ref[...].astype(jnp.float32)
    grad = grad_ref[...].astype(jnp.float32)
    for j in range(GROUPS):
        q_rows = spread(query, j, mask)
        g_rows = spread(grad, j, mask)
        gq_ref[j, 0:LANES] = g_rows.astype(jnp.bfloat16)
        gq_ref[j, LANES : 2 * LANES] = q_rows.astype(jnp.bfloat16)
        q_cols = q_rows.T
        g_cols = g_rows.T
        x_cols = spread(cells, j, mask).T
        qt_ref[j] = q_cols.astype(jnp.bfloat16)
        gt_ref[j] = g_cols.astype(jnp.bfloat16)
        xt_ref[j] = x_cols
        self_ref[0:1, j * LANES : (j + 1) * LANES] = jnp.sum(q_cols * x_cols, axis=0, keepdims=True)
        self_ref[1:2, j * LANES : (j + 1) * LANES] = jnp.sum(g_cols * x_cols, axis=0, keepdims=True)
        ot_ref[j * LANES : (j + 1) * LANES, :] = (
            outer_ref[:, j * LANES : (j + 1) * LANES].astype(jnp.float32).T.astype(jnp.bfloat16)
        )


def prepare_cells(cells, grad, probe, outer):
    width = cells.shape[1]
    hidden = outer.shape[0]
    return pl.pallas_call(
        cells_kernel,
        out_shape=(
            jax.ShapeDtypeStruct((GROUPS, LANES, LANES), jnp.bfloat16),
            jax.ShapeDtypeStruct((GROUPS, LANES, LANES), jnp.bfloat16),
            jax.ShapeDtypeStruct((GROUPS, LANES, LANES), jnp.float32),
            jax.ShapeDtypeStruct((GROUPS, 2 * LANES, LANES), jnp.bfloat16),
            jax.ShapeDtypeStruct((2, width), jnp.float32),
            jax.ShapeDtypeStruct((width, hidden), jnp.bfloat16),
        ),
        name="prepare_cells",
    )(cells, grad, probe, outer)


def contract_rows(left, right):
    return lax.dot_general(left, right, (((0,), (0,)), ((), ())), preferred_element_type=jnp.float32)


def tile_kernel(
    live_ref, recv_ref, qt_ref, gt_ref, xt_ref, gq_ref, self_ref, norm_ref, inner_ref, outer_ref, ot_ref,
    state_ref, grads_ref,
    x_s, f_s, p_s, d_s, h_s, m_s, l_s, peak_s, up_s, row_s, in_s, out_s, sem,
):
    n_src, cap, block_len, _ = recv_ref.shape
    n_slots = n_src * cap
    rows = CHUNK_BLOCKS * block_len
    f32 = jnp.float32
    bf16 = jnp.bfloat16

    def copy_in(src, slot, at):
        at_row = pl.multiple_of(at * block_len, block_len)
        return pltpu.make_async_copy(
            recv_ref.at[src, slot], x_s.at[pl.ds(at_row, block_len)], sem.at[at]
        )

    count = jnp.int32(0)
    for i in range(n_slots):
        live = live_ref[i]

        @pl.when(live > 0)
        def _(count=count, i=i):
            copy_in(i // cap, i % cap, count).start()

        count = count + live
    n_chunks = (count + CHUNK_BLOCKS - 1) // CHUNK_BLOCKS

    norm = norm_ref[...]
    self_score = self_ref[0:1, :] * norm
    m_s[...] = self_score
    l_s[...] = jnp.ones_like(l_s)
    up_s[...] = jnp.zeros_like(up_s)
    in_s[...] = jnp.zeros_like(in_s)
    out_s[...] = jnp.zeros_like(out_s)

    def forward(k, carry):
        for i in range(CHUNK_BLOCKS):
            at = k * CHUNK_BLOCKS + i

            @pl.when(at < count)
            def _():
                copy_in(0, 0, at).wait()

            @pl.when(at >= count)
            def _():
                at_row = pl.multiple_of(at * block_len, block_len)
                x_s[pl.ds(at_row, block_len), :] = jnp.zeros((block_len, x_s.shape[1]), bf16)

        start = pl.multiple_of(k * rows, rows)
        here = pl.ds(start, rows)
        pre = jnp.dot(x_s[here, :], inner_ref[...], preferred_element_type=f32)
        gate = 1.0 / (1.0 + jnp.exp(-pre))
        hidden = (pre * gate).astype(bf16)
        d_s[here, :] = gate * (1.0 + pre * (1.0 - gate))
        h_s[here, :] = hidden
        inside = lax.broadcasted_iota(jnp.int32, (rows, LANES), 0) < count * block_len - start
        for j in range(GROUPS):
            cols = pl.ds(j * LANES, LANES)
            feat = jnp.dot(hidden, outer_ref[:, cols], preferred_element_type=f32).astype(bf16)
            f_s[here, cols] = feat
            scores = jnp.dot(feat, qt_ref[j], preferred_element_type=f32) * norm[:, j * LANES : (j + 1) * LANES]
            scores = jnp.where(inside, scores, -jnp.inf)
            old = m_s[:, cols]
            peak = jnp.maximum(old, jnp.max(scores, axis=0, keepdims=True))
            fade = jnp.exp(old - peak)
            terms = jnp.exp(scores - peak)
            p_s[here, cols] = terms
            m_s[:, cols] = peak
            peak_s[k, :, cols] = peak
            l_s[:, cols] = l_s[:, cols] * fade + jnp.sum(terms, axis=0, keepdims=True)
            up_s[j] = up_s[j] * fade + contract_rows(feat, terms.astype(bf16))
        return carry

    lax.fori_loop(0, n_chunks, forward, 0)

    mask = block_mask()
    inverse = 1.0 / l_s[...]
    peak = m_s[...]
    self_prob = jnp.exp(self_score - peak) * inverse
    self_weight = self_prob.astype(bf16).astype(f32)
    for j in range(GROUPS):
        cols = slice(j * LANES, (j + 1) * LANES)
        update = jnp.where(mask, up_s[j] * inverse[:, cols], 0.0)
        row_s[:, cols] = (
            jnp.sum(update * gt_ref[j].astype(f32), axis=0, keepdims=True)
            + self_prob[:, cols] * self_ref[1:2, cols]
        )
        x_cols = xt_ref[j]
        state = (x_cols + (update + self_weight[:, cols] * x_cols)).T
        total = state[0:CHANNELS_PER_ATT]
        for h in range(1, LANES // CHANNELS_PER_ATT):
            total = total + state[h * CHANNELS_PER_ATT : (h + 1) * CHANNELS_PER_ATT]
        state_ref[:, cols] = total.astype(bf16)

    row_total = row_s[...]

    def backward(k, carry):
        start = pl.multiple_of(k * rows, rows)
        here = pl.ds(start, rows)
        scale = jnp.exp(peak_s[k] - peak) * inverse
        scaled = scale * norm
        hidden = h_s[here, :]
        hidden_grad = jnp.zeros((rows, LANES), f32)
        for j in range(GROUPS):
            cols = slice(j * LANES, (j + 1) * LANES)
            terms = p_s[here, cols]
            weights = (terms * scale[:, cols]).astype(bf16)
            weight_grad = jnp.dot(f_s[here, cols], gt_ref[j], preferred_element_type=f32)
            logit_grad = ((terms * scaled[:, cols]) * (weight_grad - row_total[:, cols])).astype(bf16)
            feat_grad = jnp.dot(
                jnp.concatenate([weights, logit_grad], axis=1), gq_ref[j], preferred_element_type=f32
            ).astype(bf16)
            hidden_grad = hidden_grad + jnp.dot(feat_grad, ot_ref[cols, :], preferred_element_type=f32)
            out_s[:, cols] = out_s[:, cols] + contract_rows(hidden, feat_grad)
        hidden_grad = (hidden_grad * d_s[here, :]).astype(bf16)
        in_s[...] = in_s[...] + contract_rows(x_s[here, :], hidden_grad)
        return carry

    lax.fori_loop(0, n_chunks, backward, 0)
    grads_ref[:, 0 : in_s.shape[1]] = in_s[...].astype(bf16)
    grads_ref[:, in_s.shape[1] :] = out_s[...].astype(bf16)


def tile_step(live, recv, qt, gt, xt, gq, self_dots, norm, inner, outer, ot, n_cells):
    n_src, cap, block_len, obs_width = recv.shape
    hidden, width = outer.shape
    n_slots = n_src * cap
    n_tokens = n_slots * block_len
    n_chunks = n_slots // CHUNK_BLOCKS
    vmem = pl.BlockSpec(memory_space=pltpu.VMEM)
    return pl.pallas_call(
        tile_kernel,
        out_shape=(
            jax.ShapeDtypeStruct((n_cells, width), jnp.bfloat16),
            jax.ShapeDtypeStruct((obs_width, hidden + width), jnp.bfloat16),
        ),
        in_specs=[pl.BlockSpec(memory_space=pltpu.SMEM), pl.BlockSpec(memory_space=pl.ANY)] + [vmem] * 9,
        out_specs=(vmem, vmem),
        scratch_shapes=[
            pltpu.VMEM((n_tokens, obs_width), jnp.bfloat16),
            pltpu.VMEM((n_tokens, width), jnp.bfloat16),
            pltpu.VMEM((n_tokens, width), jnp.float32),
            pltpu.VMEM((n_tokens, hidden), jnp.float32),
            pltpu.VMEM((n_tokens, hidden), jnp.bfloat16),
            pltpu.VMEM((1, width), jnp.float32),
            pltpu.VMEM((1, width), jnp.float32),
            pltpu.VMEM((n_chunks, 1, width), jnp.float32),
            pltpu.VMEM((GROUPS, LANES, LANES), jnp.float32),
            pltpu.VMEM((1, width), jnp.float32),
            pltpu.VMEM((obs_width, hidden), jnp.float32),
            pltpu.VMEM((hidden, width), jnp.float32),
            pltpu.SemaphoreType.DMA((n_slots,)),
        ],
        compiler_params=pltpu.CompilerParams(vmem_limit_bytes=50 * 1024 * 1024),
        name="tile_step",
    )(live, recv, qt, gt, xt, gq, self_dots, norm, inner, outer, ot)


def reduce_everywhere(grads):
    n_rows, n_cols = grads.shape
    ring = ("lon", "mem")
    count = lax.axis_size("lon") * lax.axis_size("mem")
    lat_count = lax.axis_size("lat")
    pieces = lax.all_to_all(
        grads.reshape(count, n_rows // count, n_cols), ring, split_axis=0, concat_axis=0, tiled=True
    )
    part = jnp.sum(pieces.astype(jnp.float32), axis=0)
    own = part.astype(jnp.bfloat16)
    parts = [own.astype(jnp.float32)]
    for shift in range(1, lat_count):
        pairs = [(i, (i + shift) % lat_count) for i in range(lat_count)]
        parts.append(lax.ppermute(own, "lat", pairs).astype(jnp.float32))
    while len(parts) > 1:
        half = len(parts) // 2
        parts = [parts[i] + parts[i + half] for i in range(half)]
    total = parts[0].astype(jnp.bfloat16)
    whole = lax.all_to_all(
        jnp.broadcast_to(total[None], (count,) + total.shape), ring, split_axis=0, concat_axis=0, tiled=True
    )
    return whole.reshape(n_rows, n_cols)


def per_device(
    measured_inputs,
    target_sector,
    hidden_member_fields,
    analysis_adjoint,
    inner_perceptron_coeffs,
    outer_perceptron_coeffs,
    probe_projector,
    logit_sharpness,
    adjacent_channel_coeffs,
):
    lon_count = lax.axis_size("lon")
    lat_count = lax.axis_size("lat")
    block_count = target_sector.shape[0]
    model_width = hidden_member_fields.shape[3]
    hidden_width = inner_perceptron_coeffs.shape[1]
    cell_rows = hidden_member_fields.shape[1]
    cell_cols = hidden_member_fields.shape[2]
    n_cells = cell_rows * cell_cols
    cap_slots = max(2, 2 * block_count // lon_count)
    send_blocks = pack_blocks(target_sector, measured_inputs, lon_count, cap_slots)
    obs_blocks = lax.all_to_all(send_blocks, "lon", split_axis=0, concat_axis=0, tiled=True)
    cot_padded = extended(analysis_adjoint[0], (("lat", 0), ("lon", 1)), 1)
    lat_index = lax.axis_index("lat")
    keep_rows = jnp.ones((cell_rows + 2,), jnp.float32)
    keep_rows = keep_rows.at[0].set(jnp.where(lat_index > 0, 1.0, 0.0))
    keep_rows = keep_rows.at[cell_rows + 1].set(jnp.where(lat_index < lat_count - 1, 1.0, 0.0))
    hidden_field_adjoint = (
        mix_local(cot_padded, keep_rows, adjacent_channel_coeffs, -1)
        .astype(jnp.bfloat16)
        .reshape(n_cells, model_width)
    )
    grid_point_entries = hidden_member_fields.reshape(n_cells, model_width)
    prepared = prepare_cells(
        grid_point_entries, hidden_field_adjoint, probe_projector, outer_perceptron_coeffs
    )
    qt, gt, xt, gq, self_dots, ot = prepared
    norm = jnp.repeat(logit_sharpness / math.sqrt(CHANNELS_PER_ATT), n_cells)[None, :]
    live = (obs_blocks[:, :, 0, 0] < MARK / 2).astype(jnp.int32).reshape(-1)
    revised_analysis, grads = tile_step(
        live, obs_blocks, qt, gt, xt, gq, self_dots, norm,
        inner_perceptron_coeffs, outer_perceptron_coeffs, ot, n_cells,
    )
    grads = reduce_everywhere(grads)
    state_grid = revised_analysis.reshape(cell_rows, cell_cols, model_width)
    state_padded = extended(state_grid, (("lat", 0), ("lon", 1)), 1)
    analysis = (
        mix_local(state_padded, keep_rows, adjacent_channel_coeffs, 1)
        .astype(jnp.bfloat16)
        .reshape(hidden_member_fields.shape)
    )
    grads = grads.astype(jnp.float32)
    return (analysis, grads[:, :hidden_width], grads[:, hidden_width:])


def solution(mesh):
    in_specs = (
        P(("lat", "lon", "mem"), None, None),
        P(("lat", "lon", "mem")),
        P("mem", "lat", "lon", None),
        P("mem", "lat", "lon", None),
        P(),
        P(),
        P(),
        P(),
        P(),
    )
    out_specs = (P("mem", "lat", "lon", None), P(), P())
    return jax.shard_map(
        per_device, mesh=mesh, in_specs=in_specs, out_specs=out_specs, check_vma=False
    )
```

```python
import math

import jax
import jax.numpy as jnp
from jax import lax
from jax.experimental import pallas as pl
from jax.experimental.pallas import tpu as pltpu
from jax.sharding import PartitionSpec as P

HEADS = 12
CHANNELS_PER_ATT = 64
GROUPS = 3
LANES = 256
CHUNK_BLOCKS = 4
MARK = 512.0


NEIGHBOURS = ((-1, -1), (-1, 0), (-1, 1), (0, -1), (0, 1), (1, -1), (1, 0), (1, 1))


def extended(block, sides, width):
    for axis, dim in sides:
        count = lax.axis_size(axis)
        forward = [(i, i + 1) for i in range(count - 1)]
        forward.append((count - 1, 0))
        backward = [(target, source) for source, target in forward]
        low = lax.ppermute(
            lax.slice_in_dim(block, block.shape[dim] - width, None, axis=dim), axis, forward
        )
        high = lax.ppermute(lax.slice_in_dim(block, 0, width, axis=dim), axis, backward)
        block = jnp.concatenate([low, block, high], axis=dim)
    return block


def mix_local(padded, keep_rows, adjacent_channel_coeffs, direction):
    values = padded.astype(jnp.float32) * keep_rows
    n_rows = padded.shape[0] - 2
    n_cols = padded.shape[1] - 2
    total = values[1 : 1 + n_rows, 1 : 1 + n_cols]
    for offset_idx, (row_step, col_step) in enumerate(NEIGHBOURS):
        row_start = 1 + direction * row_step
        col_start = 1 + direction * col_step
        total = (
            total
            + adjacent_channel_coeffs[offset_idx]
            * values[row_start : row_start + n_rows, col_start : col_start + n_cols]
        )
    return total


def pack_kernel(target_ref, blocks_ref, send_ref, count_ref, mark_ref, sem):
    n_blocks = blocks_ref.shape[0]
    n_dest = send_ref.shape[0]
    cap = send_ref.shape[1]
    mark_ref[...] = jnp.full(mark_ref.shape, MARK, mark_ref.dtype)
    for d in range(n_dest):
        count_ref[d] = 0

    def copy_of(b, dest, slot):
        return pltpu.make_async_copy(blocks_ref.at[b], send_ref.at[dest, slot], sem.at[b])

    for b in range(n_blocks):
        dest = target_ref[b]
        slot = count_ref[dest]
        count_ref[dest] = slot + 1
        copy_of(b, dest, slot).start()

    def mark_of(d, slot):
        return pltpu.make_async_copy(
            mark_ref, send_ref.at[d, slot, pl.ds(0, mark_ref.shape[0])], sem.at[n_blocks + d * cap + slot]
        )

    for d in range(n_dest):
        for slot in range(cap):

            @pl.when(count_ref[d] <= slot)
            def _():
                mark_of(d, slot).start()

    for b in range(n_blocks):
        copy_of(b, 0, 0).wait()
    for d in range(n_dest):
        for slot in range(cap):

            @pl.when(count_ref[d] <= slot)
            def _():
                mark_of(d, slot).wait()


def pack_blocks(target_sector, blocks, n_dest, cap):
    n_blocks, block_len, width = blocks.shape
    return pl.pallas_call(
        pack_kernel,
        out_shape=jax.ShapeDtypeStruct((n_dest, cap, block_len, width), blocks.dtype),
        in_specs=[
            pl.BlockSpec(memory_space=pltpu.SMEM),
            pl.BlockSpec(memory_space=pltpu.VMEM),
        ],
        out_specs=pl.BlockSpec(memory_space=pltpu.HBM),
        scratch_shapes=[
            pltpu.SMEM((n_dest,), jnp.int32),
            pltpu.VMEM((16, width), blocks.dtype),
            pltpu.SemaphoreType.DMA((n_blocks + n_dest * cap,)),
        ],
        compiler_params=pltpu.CompilerParams(vmem_limit_bytes=4 * 1024 * 1024),
        name="pack_blocks",
    )(target_sector, blocks)


def block_mask():
    rows = lax.broadcasted_iota(jnp.int32, (LANES, LANES), 0) // CHANNELS_PER_ATT
    cols = lax.broadcasted_iota(jnp.int32, (LANES, LANES), 1) // CHANNELS_PER_ATT
    return rows == cols


def spread(values, group, mask):
    part = values[:, group * LANES : (group + 1) * LANES].astype(jnp.float32)
    return jnp.where(mask, jnp.concatenate([part] * (LANES // CHANNELS_PER_ATT), axis=0), 0.0)


def table_rows(kind, j):
    start = {"q": 0, "g": GROUPS, "gq": 2 * GROUPS, "o": 4 * GROUPS}[kind] + (2 * j if kind == "gq" else j)
    return slice(start * LANES, (start + (2 if kind == "gq" else 1)) * LANES)


def cells_kernel(cells_ref, grad_ref, probe_ref, outer_ref, table_ref, xt_ref, self_ref):
    mask = block_mask()
    query = jnp.dot(cells_ref[...], probe_ref[...], preferred_element_type=jnp.float32)
    query = query.astype(jnp.bfloat16).astype(jnp.float32)
    cells = cells_ref[...].astype(jnp.float32)
    grad = grad_ref[...].astype(jnp.float32)
    for j in range(GROUPS):
        q_rows = spread(query, j, mask)
        g_rows = spread(grad, j, mask)
        table_ref[table_rows("gq", j), :] = jnp.concatenate([g_rows, q_rows], axis=0).astype(jnp.bfloat16)
        q_cols = q_rows.T
        g_cols = g_rows.T
        x_cols = spread(cells, j, mask).T
        table_ref[table_rows("q", j), :] = q_cols.astype(jnp.bfloat16)
        table_ref[table_rows("g", j), :] = g_cols.astype(jnp.bfloat16)
        xt_ref[j] = x_cols
        self_ref[0:1, j * LANES : (j + 1) * LANES] = jnp.sum(q_cols * x_cols, axis=0, keepdims=True)
        self_ref[1:2, j * LANES : (j + 1) * LANES] = jnp.sum(g_cols * x_cols, axis=0, keepdims=True)
        table_ref[table_rows("o", j), :] = (
            outer_ref[:, j * LANES : (j + 1) * LANES].astype(jnp.float32).T.astype(jnp.bfloat16)
        )


def prepare_cells(cells, grad, probe, outer):
    width = cells.shape[1]
    hidden = outer.shape[0]
    return pl.pallas_call(
        cells_kernel,
        out_shape=(
            jax.ShapeDtypeStruct((5 * GROUPS * LANES, hidden), jnp.bfloat16),
            jax.ShapeDtypeStruct((GROUPS, LANES, LANES), jnp.float32),
            jax.ShapeDtypeStruct((2, width), jnp.float32),
        ),
        compiler_params=pltpu.CompilerParams(vmem_limit_bytes=12 * 1024 * 1024),
        name="prepare_cells",
    )(cells, grad, probe, outer)


def contract_rows(left, right):
    return lax.dot_general(left, right, (((0,), (0,)), ((), ())), preferred_element_type=jnp.float32)


def tile_kernel(
    recv_ref, self_ref, norm_ref, inner_ref, outer_ref, table_ref, xt_ref,
    state_ref, grads_ref,
    x_s, f_s, p_s, d_s, h_s, m_s, l_s, peak_s, up_s, row_s, in_s, out_s, order_s, live_v, live_s, sem,
):
    n_slots, block_len, _ = recv_ref.shape
    rows = CHUNK_BLOCKS * block_len
    f32 = jnp.float32
    bf16 = jnp.bfloat16

    for i in range(n_slots):
        head = recv_ref[i, 0:16, 0:128].astype(f32)
        live_v[i : i + 1, :] = jnp.where(head[0:1, :] < MARK / 2, 1, 0)
    flags = pltpu.make_async_copy(live_v, live_s, sem.at[0])
    flags.start()
    l_s[...] = jnp.ones_like(l_s)
    up_s[...] = jnp.zeros_like(up_s)
    in_s[...] = jnp.zeros_like(in_s)
    out_s[...] = jnp.zeros_like(out_s)
    flags.wait()
    count = jnp.int32(0)
    for i in range(n_slots):
        order_s[count] = i
        count = count + live_s[i, 0]
    n_chunks = (count + CHUNK_BLOCKS - 1) // CHUNK_BLOCKS

    norm = norm_ref[...]
    self_score = self_ref[0:1, :] * norm
    m_s[...] = self_score

    def forward(k, carry):
        for i in range(CHUNK_BLOCKS):
            at = k * CHUNK_BLOCKS + i
            at_row = pl.ds(pl.multiple_of(at * block_len, block_len), block_len)

            @pl.when(at < count)
            def _():
                x_s[at_row, :] = recv_ref[order_s[at]]

            @pl.when(at >= count)
            def _():
                x_s[at_row, :] = jnp.zeros((block_len, x_s.shape[1]), bf16)

        start = pl.multiple_of(k * rows, rows)
        here = pl.ds(start, rows)
        pre = jnp.dot(x_s[here, :], inner_ref[...], preferred_element_type=f32)
        gate = 1.0 / (1.0 + jnp.exp(-pre))
        hidden = (pre * gate).astype(bf16)
        d_s[here, :] = gate * (1.0 + pre * (1.0 - gate))
        h_s[here, :] = hidden
        inside = lax.broadcasted_iota(jnp.int32, (rows, LANES), 0) < count * block_len - start
        for j in range(GROUPS):
            cols = pl.ds(j * LANES, LANES)
            feat = jnp.dot(hidden, outer_ref[:, cols], preferred_element_type=f32).astype(bf16)
            f_s[here, cols] = feat
            scores = jnp.dot(feat, table_ref[table_rows("q", j), :], preferred_element_type=f32) * norm[:, j * LANES : (j + 1) * LANES]
            scores = jnp.where(inside, scores, -jnp.inf)
            old = m_s[:, cols]
            peak = jnp.maximum(old, jnp.max(scores, axis=0, keepdims=True))
            fade = jnp.exp(old - peak)
            terms = jnp.exp(scores - peak)
            p_s[here, cols] = terms
            m_s[:, cols] = peak
            peak_s[k, :, cols] = peak
            l_s[:, cols] = l_s[:, cols] * fade + jnp.sum(terms, axis=0, keepdims=True)
            up_s[j] = up_s[j] * fade + contract_rows(feat, terms.astype(bf16))
        return carry

    lax.fori_loop(0, n_chunks, forward, 0)

    mask = block_mask()
    inverse = 1.0 / l_s[...]
    peak = m_s[...]
    self_prob = jnp.exp(self_score - peak) * inverse
    self_weight = self_prob.astype(bf16).astype(f32)
    for j in range(GROUPS):
        cols = slice(j * LANES, (j + 1) * LANES)
        update = jnp.where(mask, up_s[j] * inverse[:, cols], 0.0)
        row_s[:, cols] = (
            jnp.sum(update * table_ref[table_rows("g", j), :].astype(f32), axis=0, keepdims=True)
            + self_prob[:, cols] * self_ref[1:2, cols]
        )
        x_cols = xt_ref[j]
        state = (x_cols + (update + self_weight[:, cols] * x_cols)).T
        total = state[0:CHANNELS_PER_ATT]
        for h in range(1, LANES // CHANNELS_PER_ATT):
            total = total + state[h * CHANNELS_PER_ATT : (h + 1) * CHANNELS_PER_ATT]
        state_ref[:, cols] = total.astype(bf16)

    row_total = row_s[...]

    def backward(k, carry):
        start = pl.multiple_of(k * rows, rows)
        here = pl.ds(start, rows)
        scale = jnp.exp(peak_s[k] - peak) * inverse
        scaled = scale * norm
        hidden = h_s[here, :]
        hidden_grad = jnp.zeros((rows, LANES), f32)
        for j in range(GROUPS):
            cols = slice(j * LANES, (j + 1) * LANES)
            terms = p_s[here, cols]
            weights = (terms * scale[:, cols]).astype(bf16)
            weight_grad = jnp.dot(
                f_s[here, cols], table_ref[table_rows("g", j), :], preferred_element_type=f32
            )
            logit_grad = ((terms * scaled[:, cols]) * (weight_grad - row_total[:, cols])).astype(bf16)
            feat_grad = jnp.dot(
                jnp.concatenate([weights, logit_grad], axis=1),
                table_ref[table_rows("gq", j), :],
                preferred_element_type=f32,
            ).astype(bf16)
            hidden_grad = hidden_grad + jnp.dot(
                feat_grad, table_ref[table_rows("o", j), :], preferred_element_type=f32
            )
            out_s[:, cols] = out_s[:, cols] + contract_rows(hidden, feat_grad)
        hidden_grad = (hidden_grad * d_s[here, :]).astype(bf16)
        in_s[...] = in_s[...] + contract_rows(x_s[here, :], hidden_grad)
        return carry

    lax.fori_loop(0, n_chunks, backward, 0)
    grads_ref[:, 0 : in_s.shape[1]] = in_s[...].astype(bf16)
    grads_ref[:, in_s.shape[1] :] = out_s[...].astype(bf16)


def tile_step(recv, table, xt, self_dots, norm, inner, outer, n_cells):
    n_slots, block_len, obs_width = recv.shape
    hidden, width = outer.shape
    n_tokens = n_slots * block_len
    n_chunks = n_slots // CHUNK_BLOCKS
    vmem = pl.BlockSpec(memory_space=pltpu.VMEM)
    return pl.pallas_call(
        tile_kernel,
        out_shape=(
            jax.ShapeDtypeStruct((n_cells, width), jnp.bfloat16),
            jax.ShapeDtypeStruct((obs_width, hidden + width), jnp.bfloat16),
        ),
        in_specs=[vmem] * 7,
        out_specs=(vmem, vmem),
        scratch_shapes=[
            pltpu.VMEM((n_tokens, obs_width), jnp.bfloat16),
            pltpu.VMEM((n_tokens, width), jnp.bfloat16),
            pltpu.VMEM((n_tokens, width), jnp.float32),
            pltpu.VMEM((n_tokens, hidden), jnp.float32),
            pltpu.VMEM((n_tokens, hidden), jnp.bfloat16),
            pltpu.VMEM((1, width), jnp.float32),
            pltpu.VMEM((1, width), jnp.float32),
            pltpu.VMEM((n_chunks, 1, width), jnp.float32),
            pltpu.VMEM((GROUPS, LANES, LANES), jnp.float32),
            pltpu.VMEM((1, width), jnp.float32),
            pltpu.VMEM((obs_width, hidden), jnp.float32),
            pltpu.VMEM((hidden, width), jnp.float32),
            pltpu.SMEM((n_slots + 1,), jnp.int32),
            pltpu.VMEM((n_slots, 128), jnp.int32),
            pltpu.SMEM((n_slots, 128), jnp.int32),
            pltpu.SemaphoreType.DMA((1,)),
        ],
        compiler_params=pltpu.CompilerParams(vmem_limit_bytes=44 * 1024 * 1024),
        name="tile_step",
    )(recv, self_dots, norm, inner, outer, table, xt)


def reduce_everywhere(grads):
    n_rows, n_cols = grads.shape
    ring = ("lon", "mem")
    count = lax.axis_size("lon") * lax.axis_size("mem")
    lat_count = lax.axis_size("lat")
    pieces = lax.all_to_all(
        grads.reshape(count, n_rows // count, n_cols), ring, split_axis=0, concat_axis=0, tiled=True
    )
    part = jnp.sum(pieces.astype(jnp.float32), axis=0)
    copies = jnp.broadcast_to(part.astype(jnp.bfloat16)[None], (lat_count,) + part.shape)
    peers = lax.all_to_all(copies, "lat", split_axis=0, concat_axis=0, tiled=True)
    total = jnp.sum(peers.astype(jnp.float32), axis=0).astype(jnp.bfloat16)
    whole = lax.all_to_all(
        jnp.broadcast_to(total[None], (count,) + total.shape), ring, split_axis=0, concat_axis=0, tiled=True
    )
    return whole.reshape(n_rows, n_cols)


def per_device(
    measured_inputs,
    target_sector,
    hidden_member_fields,
    analysis_adjoint,
    inner_perceptron_coeffs,
    outer_perceptron_coeffs,
    probe_projector,
    logit_sharpness,
    adjacent_channel_coeffs,
):
    lon_count = lax.axis_size("lon")
    lat_count = lax.axis_size("lat")
    block_count = target_sector.shape[0]
    model_width = hidden_member_fields.shape[3]
    hidden_width = inner_perceptron_coeffs.shape[1]
    cell_rows = hidden_member_fields.shape[1]
    cell_cols = hidden_member_fields.shape[2]
    n_cells = cell_rows * cell_cols
    cap_slots = max(2, 2 * block_count // lon_count)
    send_blocks = pack_blocks(target_sector, measured_inputs, lon_count, cap_slots)
    obs_blocks = lax.all_to_all(send_blocks, "lon", split_axis=0, concat_axis=0, tiled=True)
    cot_padded = extended(analysis_adjoint[0], (("lat", 0), ("lon", 1)), 1)
    lat_index = lax.axis_index("lat")
    row_ids = lax.broadcasted_iota(jnp.int32, (cell_rows + 2, 1, 1), 0)
    outside = ((row_ids == 0) & (lat_index == 0)) | (
        (row_ids == cell_rows + 1) & (lat_index == lat_count - 1)
    )
    keep_rows = jnp.where(outside, 0.0, 1.0)
    hidden_field_adjoint = (
        mix_local(cot_padded, keep_rows, adjacent_channel_coeffs, -1)
        .astype(jnp.bfloat16)
        .reshape(n_cells, model_width)
    )
    grid_point_entries = hidden_member_fields.reshape(n_cells, model_width)
    prepared = prepare_cells(
        grid_point_entries, hidden_field_adjoint, probe_projector, outer_perceptron_coeffs
    )
    table, xt, self_dots = prepared
    norm = jnp.repeat(logit_sharpness / math.sqrt(CHANNELS_PER_ATT), n_cells)[None, :]
    revised_analysis, grads = tile_step(
        obs_blocks.reshape((-1,) + obs_blocks.shape[2:]), table, xt, self_dots, norm,
        inner_perceptron_coeffs, outer_perceptron_coeffs, n_cells,
    )
    grads = reduce_everywhere(grads)
    state_grid = revised_analysis.reshape(cell_rows, cell_cols, model_width)
    state_padded = extended(state_grid, (("lat", 0), ("lon", 1)), 1)
    analysis = (
        mix_local(state_padded, keep_rows, adjacent_channel_coeffs, 1)
        .astype(jnp.bfloat16)
        .reshape(hidden_member_fields.shape)
    )
    grads = grads.astype(jnp.float32)
    return (analysis, grads[:, :hidden_width], grads[:, hidden_width:])


def solution(mesh):
    in_specs = (
        P(("lat", "lon", "mem"), None, None),
        P(("lat", "lon", "mem")),
        P("mem", "lat", "lon", None),
        P("mem", "lat", "lon", None),
        P(),
        P(),
        P(),
        P(),
        P(),
    )
    out_specs = (P("mem", "lat", "lon", None), P(), P())
    return jax.shard_map(
        per_device, mesh=mesh, in_specs=in_specs, out_specs=out_specs, check_vma=False
    )
```

```python
import math

import jax
import jax.numpy as jnp
from jax import lax
from jax.experimental import pallas as pl
from jax.experimental.pallas import tpu as pltpu
from jax.sharding import PartitionSpec as P


CHANNELS_PER_ATT = 64
GROUPS = 3
LANES = 256
CHUNK_BLOCKS = 8
PIECE_BLOCKS = 8
MARK = 512.0


NEIGHBOURS = ((-1, -1), (-1, 0), (-1, 1), (0, -1), (0, 1), (1, -1), (1, 0), (1, 1))


def extended(block, sides, width):
    for axis, dim in sides:
        count = lax.axis_size(axis)
        forward = [(i, i + 1) for i in range(count - 1)]
        forward.append((count - 1, 0))
        backward = [(target, source) for source, target in forward]
        low = lax.ppermute(
            lax.slice_in_dim(block, block.shape[dim] - width, None, axis=dim), axis, forward
        )
        high = lax.ppermute(lax.slice_in_dim(block, 0, width, axis=dim), axis, backward)
        block = jnp.concatenate([low, block, high], axis=dim)
    return block


def mix_local(padded, keep_rows, adjacent_channel_coeffs, direction):
    values = padded.astype(jnp.float32) * keep_rows
    n_rows = padded.shape[0] - 2
    n_cols = padded.shape[1] - 2
    total = values[1 : 1 + n_rows, 1 : 1 + n_cols]
    for offset_idx, (row_step, col_step) in enumerate(NEIGHBOURS):
        row_start = 1 + direction * row_step
        col_start = 1 + direction * col_step
        total = (
            total
            + adjacent_channel_coeffs[offset_idx]
            * values[row_start : row_start + n_rows, col_start : col_start + n_cols]
        )
    return total


def pack_kernel(target_ref, blocks_ref, send_ref, count_ref, stage_ref, mark_ref, in_sem, out_sem, mark_sem):
    n_blocks = blocks_ref.shape[0]
    n_dest = send_ref.shape[0]
    cap = send_ref.shape[1]
    loads = [pltpu.make_async_copy(blocks_ref.at[b], stage_ref.at[b], in_sem.at[b]) for b in range(n_blocks)]
    for load in loads:
        load.start()
    mark_ref[...] = jnp.full(mark_ref.shape, MARK, mark_ref.dtype)
    for d in range(n_dest):
        count_ref[d] = 0

    def copy_of(b, dest, slot):
        return pltpu.make_async_copy(stage_ref.at[b], send_ref.at[dest, slot], out_sem.at[b])

    for b in range(n_blocks):
        dest = target_ref[b]
        slot = count_ref[dest]
        count_ref[dest] = slot + 1
        loads[b].wait()
        copy_of(b, dest, slot).start()

    def mark_of(d, slot):
        return pltpu.make_async_copy(
            mark_ref, send_ref.at[d, slot, pl.ds(0, mark_ref.shape[0])], mark_sem.at[d * cap + slot]
        )

    for d in range(n_dest):
        for slot in range(cap):

            @pl.when(count_ref[d] <= slot)
            def _():
                mark_of(d, slot).start()

    for b in range(n_blocks):
        copy_of(b, 0, 0).wait()
    for d in range(n_dest):
        for slot in range(cap):

            @pl.when(count_ref[d] <= slot)
            def _():
                mark_of(d, slot).wait()


def pack_blocks(target_sector, blocks, n_dest, cap):
    n_blocks, block_len, width = blocks.shape
    return pl.pallas_call(
        pack_kernel,
        out_shape=jax.ShapeDtypeStruct((n_dest, cap, block_len, width), blocks.dtype),
        in_specs=[
            pl.BlockSpec(memory_space=pltpu.SMEM),
            pl.BlockSpec(memory_space=pl.ANY),
        ],
        out_specs=pl.BlockSpec(memory_space=pl.ANY),
        scratch_shapes=[
            pltpu.SMEM((n_dest,), jnp.int32),
            pltpu.VMEM(blocks.shape, blocks.dtype),
            pltpu.VMEM((16, width), blocks.dtype),
            pltpu.SemaphoreType.DMA((n_blocks,)),
            pltpu.SemaphoreType.DMA((n_blocks,)),
            pltpu.SemaphoreType.DMA((n_dest * cap,)),
        ],
        name="pack_blocks",
    )(target_sector, blocks)


def block_mask():
    rows = lax.broadcasted_iota(jnp.int32, (LANES, LANES), 0) // CHANNELS_PER_ATT
    cols = lax.broadcasted_iota(jnp.int32, (LANES, LANES), 1) // CHANNELS_PER_ATT
    return rows == cols


def spread(values, group, mask):
    part = values[:, group * LANES : (group + 1) * LANES].astype(jnp.float32)
    return jnp.where(mask, jnp.concatenate([part] * (LANES // CHANNELS_PER_ATT), axis=0), 0.0)


def table_rows(kind, j):
    start = {"q": 0, "g": GROUPS, "gq": 2 * GROUPS, "o": 4 * GROUPS}[kind] + (2 * j if kind == "gq" else j)
    return slice(start * LANES, (start + (2 if kind == "gq" else 1)) * LANES)


def cells_kernel(cells_ref, grad_ref, probe_ref, outer_ref, table_ref, xt_ref, self_ref):
    mask = block_mask()
    query = jnp.dot(cells_ref[...], probe_ref[...], preferred_element_type=jnp.float32)
    query = query.astype(jnp.bfloat16).astype(jnp.float32)
    cells = cells_ref[...].astype(jnp.float32)
    grad = grad_ref[...].astype(jnp.float32)
    for j in range(GROUPS):
        q_rows = spread(query, j, mask)
        g_rows = spread(grad, j, mask)
        table_ref[table_rows("gq", j), :] = jnp.concatenate([g_rows, q_rows], axis=0).astype(jnp.bfloat16)
        q_cols = q_rows.T
        g_cols = g_rows.T
        x_cols = spread(cells, j, mask).T
        table_ref[table_rows("q", j), :] = q_cols.astype(jnp.bfloat16)
        table_ref[table_rows("g", j), :] = g_cols.astype(jnp.bfloat16)
        xt_ref[j] = x_cols
        self_ref[0:1, j * LANES : (j + 1) * LANES] = jnp.sum(q_cols * x_cols, axis=0, keepdims=True)
        self_ref[1:2, j * LANES : (j + 1) * LANES] = jnp.sum(g_cols * x_cols, axis=0, keepdims=True)
        table_ref[table_rows("o", j), :] = (
            outer_ref[:, j * LANES : (j + 1) * LANES].astype(jnp.float32).T.astype(jnp.bfloat16)
        )


def prepare_cells(cells, grad, probe, outer):
    width = cells.shape[1]
    hidden = outer.shape[0]
    return pl.pallas_call(
        cells_kernel,
        out_shape=(
            jax.ShapeDtypeStruct((5 * GROUPS * LANES, hidden), jnp.bfloat16),
            jax.ShapeDtypeStruct((GROUPS, LANES, LANES), jnp.float32),
            jax.ShapeDtypeStruct((2, width), jnp.float32),
        ),
        compiler_params=pltpu.CompilerParams(vmem_limit_bytes=12 * 1024 * 1024),
        name="prepare_cells",
    )(cells, grad, probe, outer)


def contract_rows(left, right):
    return lax.dot_general(left, right, (((0,), (0,)), ((), ())), preferred_element_type=jnp.float32)


def tile_kernel(
    recv_hbm, self_ref, norm_ref, inner_ref, outer_ref, table_hbm, xt_ref,
    state_ref, grads_ref,
    recv_ref, head_ref, table_ref,
    x_s, f_s, p_s, d_s, h_s, m_s, l_s, peak_s, up_s, row_s, in_s, out_s, order_s, live_v, live_s, sem,
):
    n_slots, block_len, _ = recv_hbm.shape
    rows = CHUNK_BLOCKS * block_len
    f32 = jnp.float32
    bf16 = jnp.bfloat16

    head_copy = pltpu.make_async_copy(
        recv_hbm.at[:, pl.ds(0, head_ref.shape[1]), pl.ds(0, head_ref.shape[2])], head_ref, sem.at[1]
    )
    recv_copy = pltpu.make_async_copy(recv_hbm, recv_ref, sem.at[2])
    table_copy = pltpu.make_async_copy(table_hbm, table_ref, sem.at[3])
    head_copy.start()
    recv_copy.start()
    table_copy.start()
    l_s[...] = jnp.ones_like(l_s)
    up_s[...] = jnp.zeros_like(up_s)
    in_s[...] = jnp.zeros_like(in_s)
    out_s[...] = jnp.zeros_like(out_s)
    head_copy.wait()
    for i in range(n_slots):
        head = head_ref[i].astype(f32)
        live_v[i : i + 1, :] = jnp.where(head[0:1, :] < MARK / 2, 1, 0)
    flags = pltpu.make_async_copy(live_v, live_s, sem.at[0])
    flags.start()
    flags.wait()
    count = jnp.int32(0)
    for i in range(n_slots):
        order_s[count] = i
        count = count + live_s[i, 0]
    recv_copy.wait()
    table_copy.wait()
    n_chunks = (count + CHUNK_BLOCKS - 1) // CHUNK_BLOCKS

    norm = norm_ref[...]
    self_score = self_ref[0:1, :] * norm
    m_s[...] = self_score

    def forward(k, carry):
        for i in range(CHUNK_BLOCKS):
            at = k * CHUNK_BLOCKS + i
            at_row = pl.ds(pl.multiple_of(at * block_len, block_len), block_len)

            @pl.when(at < count)
            def _():
                x_s[at_row, :] = recv_ref[order_s[at]]

            @pl.when(at >= count)
            def _():
                x_s[at_row, :] = jnp.zeros((block_len, x_s.shape[1]), bf16)

        start = pl.multiple_of(k * rows, rows)
        piece = PIECE_BLOCKS * block_len
        n_pieces = CHUNK_BLOCKS // PIECE_BLOCKS
        at = [pl.ds(start + i * piece, piece) for i in range(n_pieces)]
        columns = [slice(j * LANES, (j + 1) * LANES) for j in range(GROUPS)]
        bias = [jnp.where(k * CHUNK_BLOCKS + i < count, 0.0, -jnp.inf) for i in range(CHUNK_BLOCKS)]
        for i in range(n_pieces):
            pre = jnp.dot(x_s[at[i], :], inner_ref[...], preferred_element_type=f32)
            gate = 1.0 / (1.0 + jnp.exp(-pre))
            hidden = (pre * gate).astype(bf16)
            d_s[at[i], :] = gate * (1.0 + pre * (1.0 - gate))
            h_s[at[i], :] = hidden
            f_s[at[i], :] = jnp.dot(hidden, outer_ref[...], preferred_element_type=f32).astype(bf16)

        def score(j, i):
            raw = jnp.dot(f_s[at[i], columns[j]], table_ref[table_rows("q", j), :], preferred_element_type=f32)
            raw = raw * norm[:, columns[j]]
            top = None
            for n in range(PIECE_BLOCKS):
                part = raw[n * block_len : (n + 1) * block_len] + bias[i * PIECE_BLOCKS + n]
                p_s[pl.ds(start + i * piece + n * block_len, block_len), columns[j]] = part
                part_top = jnp.max(part, axis=0, keepdims=True)
                top = part_top if top is None else jnp.maximum(top, part_top)
            return top

        tops = [score(0, i) for i in range(n_pieces)]
        for j in range(GROUPS):
            cols = columns[j]
            old = m_s[:, cols]
            peak = old
            for top in tops:
                peak = jnp.maximum(peak, top)
            fade = jnp.exp(old - peak)
            total = l_s[:, cols] * fade
            update = up_s[j] * fade
            tops = []
            for i in range(n_pieces):
                terms = jnp.exp(p_s[at[i], cols] - peak)
                p_s[at[i], cols] = terms
                total = total + jnp.sum(terms, axis=0, keepdims=True)
                if j + 1 < GROUPS:
                    tops.append(score(j + 1, i))
                update = update + contract_rows(f_s[at[i], cols], terms.astype(bf16))
            m_s[:, cols] = peak
            peak_s[k, :, cols] = peak
            l_s[:, cols] = total
            up_s[j] = update
        return carry

    lax.fori_loop(0, n_chunks, forward, 0)

    mask = block_mask()
    inverse = 1.0 / l_s[...]
    peak = m_s[...]
    self_prob = jnp.exp(self_score - peak) * inverse
    self_weight = self_prob.astype(bf16).astype(f32)
    for j in range(GROUPS):
        cols = slice(j * LANES, (j + 1) * LANES)
        update = jnp.where(mask, up_s[j] * inverse[:, cols], 0.0)
        row_s[:, cols] = (
            jnp.sum(update * table_ref[table_rows("g", j), :].astype(f32), axis=0, keepdims=True)
            + self_prob[:, cols] * self_ref[1:2, cols]
        )
        x_cols = xt_ref[j]
        state = (x_cols + (update + self_weight[:, cols] * x_cols)).T
        total = state[0:CHANNELS_PER_ATT]
        for h in range(1, LANES // CHANNELS_PER_ATT):
            total = total + state[h * CHANNELS_PER_ATT : (h + 1) * CHANNELS_PER_ATT]
        state_ref[:, cols] = total.astype(bf16)

    row_total = row_s[...]

    def backward(k, carry):
        start = pl.multiple_of(k * rows, rows)
        here = pl.ds(start, rows)
        scale = jnp.exp(peak_s[k] - peak) * inverse
        scaled = scale * norm
        hidden = h_s[here, :]
        hidden_grad = jnp.zeros((rows, LANES), f32)
        for j in range(GROUPS):
            cols = slice(j * LANES, (j + 1) * LANES)
            terms = p_s[here, cols]
            weights = (terms * scale[:, cols]).astype(bf16)
            weight_grad = jnp.dot(
                f_s[here, cols], table_ref[table_rows("g", j), :], preferred_element_type=f32
            )
            logit_grad = ((terms * scaled[:, cols]) * (weight_grad - row_total[:, cols])).astype(bf16)
            feat_grad = jnp.dot(
                jnp.concatenate([weights, logit_grad], axis=1),
                table_ref[table_rows("gq", j), :],
                preferred_element_type=f32,
            ).astype(bf16)
            hidden_grad = hidden_grad + jnp.dot(
                feat_grad, table_ref[table_rows("o", j), :], preferred_element_type=f32
            )
            out_s[:, cols] = out_s[:, cols] + contract_rows(hidden, feat_grad)
        hidden_grad = (hidden_grad * d_s[here, :]).astype(bf16)
        in_s[...] = in_s[...] + contract_rows(x_s[here, :], hidden_grad)
        return carry

    lax.fori_loop(0, n_chunks, backward, 0)
    grads_ref[:, 0 : in_s.shape[1]] = in_s[...].astype(bf16)
    grads_ref[:, in_s.shape[1] :] = out_s[...].astype(bf16)


def tile_step(recv, table, xt, self_dots, norm, inner, outer, n_cells):
    n_slots, block_len, obs_width = recv.shape
    hidden, width = outer.shape
    n_tokens = n_slots * block_len
    n_chunks = n_slots // CHUNK_BLOCKS
    vmem = pl.BlockSpec(memory_space=pltpu.VMEM)
    return pl.pallas_call(
        tile_kernel,
        out_shape=(
            jax.ShapeDtypeStruct((n_cells, width), jnp.bfloat16),
            jax.ShapeDtypeStruct((obs_width, hidden + width), jnp.bfloat16),
        ),
        in_specs=[pl.BlockSpec(memory_space=pl.ANY)]
        + [vmem] * 4
        + [pl.BlockSpec(memory_space=pl.ANY), vmem],
        out_specs=(vmem, vmem),
        scratch_shapes=[
            pltpu.VMEM(recv.shape, recv.dtype),
            pltpu.VMEM((n_slots, 16, 128), recv.dtype),
            pltpu.VMEM(table.shape, table.dtype),
            pltpu.VMEM((n_tokens, obs_width), jnp.bfloat16),
            pltpu.VMEM((n_tokens, width), jnp.bfloat16),
            pltpu.VMEM((n_tokens, width), jnp.float32),
            pltpu.VMEM((n_tokens, hidden), jnp.float32),
            pltpu.VMEM((n_tokens, hidden), jnp.bfloat16),
            pltpu.VMEM((1, width), jnp.float32),
            pltpu.VMEM((1, width), jnp.float32),
            pltpu.VMEM((n_chunks, 1, width), jnp.float32),
            pltpu.VMEM((GROUPS, LANES, LANES), jnp.float32),
            pltpu.VMEM((1, width), jnp.float32),
            pltpu.VMEM((obs_width, hidden), jnp.float32),
            pltpu.VMEM((hidden, width), jnp.float32),
            pltpu.SMEM((n_slots + 1,), jnp.int32),
            pltpu.VMEM((n_slots, 128), jnp.int32),
            pltpu.SMEM((n_slots, 128), jnp.int32),
            pltpu.SemaphoreType.DMA((4,)),
        ],
        compiler_params=pltpu.CompilerParams(vmem_limit_bytes=52 * 1024 * 1024),
        name="tile_step",
    )(recv, self_dots, norm, inner, outer, table, xt)


def unfold_kernel(half_ref, own_ref, other_ref, in_ref, out_ref):
    rows, _ = own_ref.shape
    hidden = in_ref.shape[1]
    own_at = pl.ds(pl.multiple_of(half_ref[0] * rows, rows), rows)
    other_at = pl.ds(pl.multiple_of((1 - half_ref[0]) * rows, rows), rows)
    in_ref[own_at, :] = own_ref[:, 0:hidden].astype(jnp.float32)
    in_ref[other_at, :] = other_ref[:, 0:hidden].astype(jnp.float32)
    out_ref[own_at, :] = own_ref[:, hidden:].astype(jnp.float32)
    out_ref[other_at, :] = other_ref[:, hidden:].astype(jnp.float32)


def unfold(half, own, other, hidden):
    rows, cols = own.shape
    vmem = pl.BlockSpec(memory_space=pltpu.VMEM)
    return pl.pallas_call(
        unfold_kernel,
        out_shape=(
            jax.ShapeDtypeStruct((2 * rows, hidden), jnp.float32),
            jax.ShapeDtypeStruct((2 * rows, cols - hidden), jnp.float32),
        ),
        in_specs=[pl.BlockSpec(memory_space=pltpu.SMEM), vmem, vmem],
        out_specs=(vmem, vmem),
        compiler_params=pltpu.CompilerParams(vmem_limit_bytes=8 * 1024 * 1024),
        name="unfold",
    )(half.reshape(1), own, other)


def reduce_everywhere(grads, hidden):
    n_rows, n_cols = grads.shape
    lon_count = lax.axis_size("lon")
    lat_count = lax.axis_size("lat")
    half = lax.axis_index("mem")
    swap = [(0, 1), (1, 0)]
    halves = grads.reshape(2, n_rows // 2, n_cols)
    mine = lax.dynamic_index_in_dim(halves, half, 0, keepdims=False).astype(jnp.float32)
    theirs = lax.ppermute(lax.dynamic_index_in_dim(halves, 1 - half, 0, keepdims=False), "mem", swap)
    pair = (mine + theirs.astype(jnp.float32)).astype(jnp.bfloat16)
    pieces = lax.all_to_all(
        pair.reshape(lon_count, n_rows // 2 // lon_count, n_cols), "lon", split_axis=0, concat_axis=0, tiled=True
    )
    part = jnp.sum(pieces.astype(jnp.float32), axis=0).astype(jnp.bfloat16)
    peers = lax.all_to_all(
        jnp.broadcast_to(part[None], (lat_count,) + part.shape), "lat", split_axis=0, concat_axis=0, tiled=True
    )
    total = jnp.sum(peers.astype(jnp.float32), axis=0).astype(jnp.bfloat16)
    own = lax.all_to_all(
        jnp.broadcast_to(total[None], (lon_count,) + total.shape), "lon", split_axis=0, concat_axis=0, tiled=True
    ).reshape(n_rows // 2, n_cols)
    other = lax.ppermute(own, "mem", swap)
    return unfold(half, own, other, hidden)


def per_device(
    measured_inputs,
    target_sector,
    hidden_member_fields,
    analysis_adjoint,
    inner_perceptron_coeffs,
    outer_perceptron_coeffs,
    probe_projector,
    logit_sharpness,
    adjacent_channel_coeffs,
):
    lon_count = lax.axis_size("lon")
    lat_count = lax.axis_size("lat")
    block_count = target_sector.shape[0]
    model_width = hidden_member_fields.shape[3]
    hidden_width = inner_perceptron_coeffs.shape[1]
    cell_rows = hidden_member_fields.shape[1]
    cell_cols = hidden_member_fields.shape[2]
    n_cells = cell_rows * cell_cols
    cap_slots = max(2, 2 * block_count // lon_count)
    send_blocks = pack_blocks(target_sector, measured_inputs, lon_count, cap_slots)
    obs_blocks = lax.all_to_all(send_blocks, "lon", split_axis=0, concat_axis=0, tiled=True)
    cot_padded = extended(analysis_adjoint[0], (("lat", 0), ("lon", 1)), 1)
    lat_index = lax.axis_index("lat")
    row_ids = lax.broadcasted_iota(jnp.int32, (cell_rows + 2, 1, 1), 0)
    outside = ((row_ids == 0) & (lat_index == 0)) | (
        (row_ids == cell_rows + 1) & (lat_index == lat_count - 1)
    )
    keep_rows = jnp.where(outside, 0.0, 1.0)
    hidden_field_adjoint = (
        mix_local(cot_padded, keep_rows, adjacent_channel_coeffs, -1)
        .astype(jnp.bfloat16)
        .reshape(n_cells, model_width)
    )
    grid_point_entries = hidden_member_fields.reshape(n_cells, model_width)
    prepared = prepare_cells(
        grid_point_entries, hidden_field_adjoint, probe_projector, outer_perceptron_coeffs
    )
    table, xt, self_dots = prepared
    norm = jnp.repeat(logit_sharpness / math.sqrt(CHANNELS_PER_ATT), n_cells)[None, :]
    revised_analysis, grads = tile_step(
        obs_blocks.reshape((-1,) + obs_blocks.shape[2:]), table, xt, self_dots, norm,
        inner_perceptron_coeffs, outer_perceptron_coeffs, n_cells,
    )
    in_grad, out_grad = reduce_everywhere(grads, hidden_width)
    state_grid = revised_analysis.reshape(cell_rows, cell_cols, model_width)
    state_padded = extended(state_grid, (("lat", 0), ("lon", 1)), 1)
    analysis = (
        mix_local(state_padded, keep_rows, adjacent_channel_coeffs, 1)
        .astype(jnp.bfloat16)
        .reshape(hidden_member_fields.shape)
    )
    return (analysis, in_grad, out_grad)


def solution(mesh):
    in_specs = (
        P(("lat", "lon", "mem"), None, None),
        P(("lat", "lon", "mem")),
        P("mem", "lat", "lon", None),
        P("mem", "lat", "lon", None),
        P(),
        P(),
        P(),
        P(),
        P(),
    )
    out_specs = (P("mem", "lat", "lon", None), P(), P())

    return jax.shard_map(per_device, mesh=mesh, in_specs=in_specs, out_specs=out_specs, check_vma=False)
```

```python
import math

import jax
import jax.numpy as jnp
from jax import lax
from jax.experimental import pallas as pl
from jax.experimental.pallas import tpu as pltpu
from jax.sharding import PartitionSpec as P


CHANNELS_PER_ATT = 64
GROUPS = 3
LANES = 256
CHUNK_BLOCKS = 8
PIECE_BLOCKS = 8
MARK = 512.0
TABLE_ROWS = 5 * GROUPS * LANES
ROOM = 40


NEIGHBOURS = ((-1, -1), (-1, 0), (-1, 1), (0, -1), (0, 1), (1, -1), (1, 0), (1, 1))


def extended(block, sides, width):
    for axis, dim in sides:
        count = lax.axis_size(axis)
        forward = [(i, i + 1) for i in range(count - 1)]
        forward.append((count - 1, 0))
        backward = [(target, source) for source, target in forward]
        low = lax.ppermute(
            lax.slice_in_dim(block, block.shape[dim] - width, None, axis=dim), axis, forward
        )
        high = lax.ppermute(lax.slice_in_dim(block, 0, width, axis=dim), axis, backward)
        block = jnp.concatenate([low, block, high], axis=dim)
    return block


def mix_local(padded, keep_rows, adjacent_channel_coeffs, direction):
    values = padded.astype(jnp.float32) * keep_rows
    n_rows = padded.shape[0] - 2
    n_cols = padded.shape[1] - 2
    total = values[1 : 1 + n_rows, 1 : 1 + n_cols]
    for offset_idx, (row_step, col_step) in enumerate(NEIGHBOURS):
        row_start = 1 + direction * row_step
        col_start = 1 + direction * col_step
        total = (
            total
            + adjacent_channel_coeffs[offset_idx]
            * values[row_start : row_start + n_rows, col_start : col_start + n_cols]
        )
    return total


def pack_kernel(target_ref, blocks_ref, send_ref, count_ref, stage_ref, mark_ref, in_sem, out_sem, mark_sem):
    n_blocks = blocks_ref.shape[0]
    n_dest = send_ref.shape[0]
    cap = send_ref.shape[1]
    loads = [pltpu.make_async_copy(blocks_ref.at[b], stage_ref.at[b], in_sem.at[b]) for b in range(n_blocks)]
    for load in loads:
        load.start()
    mark_ref[...] = jnp.full(mark_ref.shape, MARK, mark_ref.dtype)
    for d in range(n_dest):
        count_ref[d] = 0

    def copy_of(b, dest, slot):
        return pltpu.make_async_copy(stage_ref.at[b], send_ref.at[dest, slot], out_sem.at[b])

    for b in range(n_blocks):
        dest = target_ref[b]
        slot = count_ref[dest]
        count_ref[dest] = slot + 1
        loads[b].wait()
        copy_of(b, dest, slot).start()

    def mark_of(d, slot):
        return pltpu.make_async_copy(
            mark_ref, send_ref.at[d, slot, pl.ds(0, mark_ref.shape[0])], mark_sem.at[d * cap + slot]
        )

    for d in range(n_dest):
        for slot in range(cap):

            @pl.when(count_ref[d] <= slot)
            def _():
                mark_of(d, slot).start()

    for b in range(n_blocks):
        copy_of(b, 0, 0).wait()
    for d in range(n_dest):
        for slot in range(cap):

            @pl.when(count_ref[d] <= slot)
            def _():
                mark_of(d, slot).wait()


def pack_blocks(target_sector, blocks, n_dest, cap):
    n_blocks, block_len, width = blocks.shape
    return pl.pallas_call(
        pack_kernel,
        out_shape=jax.ShapeDtypeStruct((n_dest, cap, block_len, width), blocks.dtype),
        in_specs=[
            pl.BlockSpec(memory_space=pltpu.SMEM),
            pl.BlockSpec(memory_space=pl.ANY),
        ],
        out_specs=pl.BlockSpec(memory_space=pl.ANY),
        scratch_shapes=[
            pltpu.SMEM((n_dest,), jnp.int32),
            pltpu.VMEM(blocks.shape, blocks.dtype),
            pltpu.VMEM((16, width), blocks.dtype),
            pltpu.SemaphoreType.DMA((n_blocks,)),
            pltpu.SemaphoreType.DMA((n_blocks,)),
            pltpu.SemaphoreType.DMA((n_dest * cap,)),
        ],
        name="pack_blocks",
    )(target_sector, blocks)


def block_mask():
    rows = lax.broadcasted_iota(jnp.int32, (LANES, LANES), 0) // CHANNELS_PER_ATT
    cols = lax.broadcasted_iota(jnp.int32, (LANES, LANES), 1) // CHANNELS_PER_ATT
    return rows == cols


def spread(values, group, mask):
    part = values[:, group * LANES : (group + 1) * LANES].astype(jnp.float32)
    return jnp.where(mask, jnp.concatenate([part] * (LANES // CHANNELS_PER_ATT), axis=0), 0.0)


def table_rows(kind, j):
    start = {"q": 0, "g": GROUPS, "gq": 2 * GROUPS, "o": 4 * GROUPS}[kind] + (2 * j if kind == "gq" else j)
    return slice(start * LANES, (start + (2 if kind == "gq" else 1)) * LANES)


def cells_kernel(cells_ref, grad_ref, probe_ref, outer_ref, table_hbm, xt_ref, self_ref, table_ref, sem):
    mask = block_mask()
    query = jnp.dot(cells_ref[...], probe_ref[...], preferred_element_type=jnp.float32)
    query = query.astype(jnp.bfloat16).astype(jnp.float32)
    cells = cells_ref[...].astype(jnp.float32)
    grad = grad_ref[...].astype(jnp.float32)
    for j in range(GROUPS):
        q_rows = spread(query, j, mask)
        g_rows = spread(grad, j, mask)
        table_ref[table_rows("gq", j), :] = jnp.concatenate([g_rows, q_rows], axis=0).astype(jnp.bfloat16)
        q_cols = q_rows.T
        g_cols = g_rows.T
        x_cols = spread(cells, j, mask).T
        table_ref[table_rows("q", j), :] = q_cols.astype(jnp.bfloat16)
        table_ref[table_rows("g", j), :] = g_cols.astype(jnp.bfloat16)
        xt_ref[j] = x_cols
        self_ref[0:1, j * LANES : (j + 1) * LANES] = jnp.sum(q_cols * x_cols, axis=0, keepdims=True)
        self_ref[1:2, j * LANES : (j + 1) * LANES] = jnp.sum(g_cols * x_cols, axis=0, keepdims=True)
        table_ref[table_rows("o", j), :] = (
            outer_ref[:, j * LANES : (j + 1) * LANES].astype(jnp.float32).T.astype(jnp.bfloat16)
        )
    copy = pltpu.make_async_copy(table_ref, table_hbm.at[pl.ds(0, table_ref.shape[0])], sem)
    copy.start()
    copy.wait()


def prepare_cells(cells, grad, probe, outer):
    width = cells.shape[1]
    hidden = outer.shape[0]
    vmem = pl.BlockSpec(memory_space=pltpu.VMEM)
    return pl.pallas_call(
        cells_kernel,
        out_shape=(
            jax.ShapeDtypeStruct((TABLE_ROWS * ROOM, hidden), jnp.bfloat16),
            jax.ShapeDtypeStruct((GROUPS, LANES, LANES), jnp.float32),
            jax.ShapeDtypeStruct((2, width), jnp.float32),
        ),
        out_specs=(pl.BlockSpec(memory_space=pl.ANY), vmem, vmem),
        scratch_shapes=[pltpu.VMEM((TABLE_ROWS, hidden), jnp.bfloat16), pltpu.SemaphoreType.DMA],
        compiler_params=pltpu.CompilerParams(vmem_limit_bytes=12 * 1024 * 1024),
        name="prepare_cells",
    )(cells, grad, probe, outer)


def contract_rows(left, right):
    return lax.dot_general(left, right, (((0,), (0,)), ((), ())), preferred_element_type=jnp.float32)


def tile_kernel(
    half_ref, recv_hbm, self_ref, norm_ref, inner_ref, outer_ref, table_hbm, xt_ref,
    state_ref, keep_ref, give_ref,
    recv_ref, head_ref, table_ref,
    x_s, f_s, p_s, d_s, h_s, m_s, l_s, peak_s, up_s, row_s, in_s, out_s, order_s, live_v, live_s, sem,
):
    n_slots, block_len, _ = recv_hbm.shape
    rows = CHUNK_BLOCKS * block_len
    f32 = jnp.float32
    bf16 = jnp.bfloat16

    head_copy = pltpu.make_async_copy(
        recv_hbm.at[:, pl.ds(0, head_ref.shape[1]), pl.ds(0, head_ref.shape[2])], head_ref, sem.at[1]
    )
    recv_copy = pltpu.make_async_copy(recv_hbm, recv_ref, sem.at[2])
    table_copy = pltpu.make_async_copy(table_hbm.at[pl.ds(0, TABLE_ROWS)], table_ref, sem.at[3])
    head_copy.start()
    recv_copy.start()
    table_copy.start()
    l_s[...] = jnp.ones_like(l_s)
    up_s[...] = jnp.zeros_like(up_s)
    in_s[...] = jnp.zeros_like(in_s)
    out_s[...] = jnp.zeros_like(out_s)
    head_copy.wait()
    for i in range(n_slots):
        head = head_ref[i].astype(f32)
        live_v[i : i + 1, :] = jnp.where(head[0:1, :] < MARK / 2, 1, 0)
    flags = pltpu.make_async_copy(live_v, live_s, sem.at[0])
    flags.start()
    flags.wait()
    count = jnp.int32(0)
    for i in range(n_slots):
        order_s[count] = i
        count = count + live_s[i, 0]
    recv_copy.wait()
    table_copy.wait()
    n_chunks = (count + CHUNK_BLOCKS - 1) // CHUNK_BLOCKS

    norm = norm_ref[...]
    self_score = self_ref[0:1, :] * norm
    m_s[...] = self_score

    def forward(k, carry):
        for i in range(CHUNK_BLOCKS):
            at = k * CHUNK_BLOCKS + i
            at_row = pl.ds(pl.multiple_of(at * block_len, block_len), block_len)

            @pl.when(at < count)
            def _():
                x_s[at_row, :] = recv_ref[order_s[at]]

            @pl.when(at >= count)
            def _():
                x_s[at_row, :] = jnp.zeros((block_len, x_s.shape[1]), bf16)

        start = pl.multiple_of(k * rows, rows)
        piece = PIECE_BLOCKS * block_len
        n_pieces = CHUNK_BLOCKS // PIECE_BLOCKS
        at = [pl.ds(start + i * piece, piece) for i in range(n_pieces)]
        columns = [slice(j * LANES, (j + 1) * LANES) for j in range(GROUPS)]
        bias = [jnp.where(k * CHUNK_BLOCKS + i < count, 0.0, -jnp.inf) for i in range(CHUNK_BLOCKS)]
        for i in range(n_pieces):
            pre = jnp.dot(x_s[at[i], :], inner_ref[...], preferred_element_type=f32)
            gate = 1.0 / (1.0 + jnp.exp(-pre))
            hidden = (pre * gate).astype(bf16)
            d_s[at[i], :] = gate * (1.0 + pre * (1.0 - gate))
            h_s[at[i], :] = hidden
            f_s[at[i], :] = jnp.dot(hidden, outer_ref[...], preferred_element_type=f32).astype(bf16)

        def score(j, i):
            raw = jnp.dot(f_s[at[i], columns[j]], table_ref[table_rows("q", j), :], preferred_element_type=f32)
            raw = raw * norm[:, columns[j]]
            top = None
            for n in range(PIECE_BLOCKS):
                part = raw[n * block_len : (n + 1) * block_len] + bias[i * PIECE_BLOCKS + n]
                p_s[pl.ds(start + i * piece + n * block_len, block_len), columns[j]] = part
                part_top = jnp.max(part, axis=0, keepdims=True)
                top = part_top if top is None else jnp.maximum(top, part_top)
            return top

        tops = [score(0, i) for i in range(n_pieces)]
        for j in range(GROUPS):
            cols = columns[j]
            old = m_s[:, cols]
            peak = old
            for top in tops:
                peak = jnp.maximum(peak, top)
            fade = jnp.exp(old - peak)
            total = l_s[:, cols] * fade
            update = up_s[j] * fade
            tops = []
            for i in range(n_pieces):
                terms = jnp.exp(p_s[at[i], cols] - peak)
                p_s[at[i], cols] = terms
                total = total + jnp.sum(terms, axis=0, keepdims=True)
                if j + 1 < GROUPS:
                    tops.append(score(j + 1, i))
                update = update + contract_rows(f_s[at[i], cols], terms.astype(bf16))
            m_s[:, cols] = peak
            peak_s[k, :, cols] = peak
            l_s[:, cols] = total
            up_s[j] = update
        return carry

    lax.fori_loop(0, n_chunks, forward, 0)

    mask = block_mask()
    inverse = 1.0 / l_s[...]
    peak = m_s[...]
    self_prob = jnp.exp(self_score - peak) * inverse
    self_weight = self_prob.astype(bf16).astype(f32)
    for j in range(GROUPS):
        cols = slice(j * LANES, (j + 1) * LANES)
        update = jnp.where(mask, up_s[j] * inverse[:, cols], 0.0)
        row_s[:, cols] = (
            jnp.sum(update * table_ref[table_rows("g", j), :].astype(f32), axis=0, keepdims=True)
            + self_prob[:, cols] * self_ref[1:2, cols]
        )
        x_cols = xt_ref[j]
        state = (x_cols + (update + self_weight[:, cols] * x_cols)).T
        total = state[0:CHANNELS_PER_ATT]
        for h in range(1, LANES // CHANNELS_PER_ATT):
            total = total + state[h * CHANNELS_PER_ATT : (h + 1) * CHANNELS_PER_ATT]
        state_ref[:, cols] = total.astype(bf16)

    row_total = row_s[...]

    def backward(k, carry):
        start = pl.multiple_of(k * rows, rows)
        here = pl.ds(start, rows)
        scale = jnp.exp(peak_s[k] - peak) * inverse
        scaled = scale * norm
        hidden = h_s[here, :]
        hidden_grad = jnp.zeros((rows, LANES), f32)
        for j in range(GROUPS):
            cols = slice(j * LANES, (j + 1) * LANES)
            terms = p_s[here, cols]
            weights = (terms * scale[:, cols]).astype(bf16)
            weight_grad = jnp.dot(
                f_s[here, cols], table_ref[table_rows("g", j), :], preferred_element_type=f32
            )
            logit_grad = ((terms * scaled[:, cols]) * (weight_grad - row_total[:, cols])).astype(bf16)
            feat_grad = jnp.dot(
                jnp.concatenate([weights, logit_grad], axis=1),
                table_ref[table_rows("gq", j), :],
                preferred_element_type=f32,
            ).astype(bf16)
            hidden_grad = hidden_grad + jnp.dot(
                feat_grad, table_ref[table_rows("o", j), :], preferred_element_type=f32
            )
            out_s[:, cols] = out_s[:, cols] + contract_rows(hidden, feat_grad)
        hidden_grad = (hidden_grad * d_s[here, :]).astype(bf16)
        in_s[...] = in_s[...] + contract_rows(x_s[here, :], hidden_grad)
        return carry

    lax.fori_loop(0, n_chunks, backward, 0)
    n_rows = keep_ref.shape[0]
    split = in_s.shape[1]
    for dst, half in ((keep_ref, half_ref[0]), (give_ref, 1 - half_ref[0])):
        here = pl.ds(pl.multiple_of(half * n_rows, n_rows), n_rows)
        dst[:, 0:split] = in_s[here, :].astype(bf16)
        dst[:, split:] = out_s[here, :].astype(bf16)


def tile_step(half, recv, table, xt, self_dots, norm, inner, outer, n_cells):
    n_slots, block_len, obs_width = recv.shape
    hidden, width = outer.shape
    n_tokens = n_slots * block_len
    n_chunks = n_slots // CHUNK_BLOCKS
    vmem = pl.BlockSpec(memory_space=pltpu.VMEM)
    return pl.pallas_call(
        tile_kernel,
        out_shape=(
            jax.ShapeDtypeStruct((n_cells, width), jnp.bfloat16),
            jax.ShapeDtypeStruct((obs_width // 2, hidden + width), jnp.bfloat16),
            jax.ShapeDtypeStruct((obs_width // 2, hidden + width), jnp.bfloat16),
        ),
        in_specs=[pl.BlockSpec(memory_space=pltpu.SMEM), pl.BlockSpec(memory_space=pl.ANY)]
        + [vmem] * 4
        + [pl.BlockSpec(memory_space=pl.ANY), vmem],
        out_specs=(vmem, vmem, vmem),
        scratch_shapes=[
            pltpu.VMEM(recv.shape, recv.dtype),
            pltpu.VMEM((n_slots, 16, 128), recv.dtype),
            pltpu.VMEM((TABLE_ROWS, hidden), table.dtype),
            pltpu.VMEM((n_tokens, obs_width), jnp.bfloat16),
            pltpu.VMEM((n_tokens, width), jnp.bfloat16),
            pltpu.VMEM((n_tokens, width), jnp.float32),
            pltpu.VMEM((n_tokens, hidden), jnp.float32),
            pltpu.VMEM((n_tokens, hidden), jnp.bfloat16),
            pltpu.VMEM((1, width), jnp.float32),
            pltpu.VMEM((1, width), jnp.float32),
            pltpu.VMEM((n_chunks, 1, width), jnp.float32),
            pltpu.VMEM((GROUPS, LANES, LANES), jnp.float32),
            pltpu.VMEM((1, width), jnp.float32),
            pltpu.VMEM((obs_width, hidden), jnp.float32),
            pltpu.VMEM((hidden, width), jnp.float32),
            pltpu.SMEM((n_slots + 1,), jnp.int32),
            pltpu.VMEM((n_slots, 128), jnp.int32),
            pltpu.SMEM((n_slots, 128), jnp.int32),
            pltpu.SemaphoreType.DMA((4,)),
        ],
        compiler_params=pltpu.CompilerParams(vmem_limit_bytes=44 * 1024 * 1024),
        name="tile_step",
    )(half, recv, self_dots, norm, inner, outer, table, xt)


def unfold_kernel(half_ref, own_ref, other_ref, in_ref, out_ref):
    rows, _ = own_ref.shape
    hidden = in_ref.shape[1]
    own_at = pl.ds(pl.multiple_of(half_ref[0] * rows, rows), rows)
    other_at = pl.ds(pl.multiple_of((1 - half_ref[0]) * rows, rows), rows)
    in_ref[own_at, :] = own_ref[:, 0:hidden].astype(jnp.float32)
    in_ref[other_at, :] = other_ref[:, 0:hidden].astype(jnp.float32)
    out_ref[own_at, :] = own_ref[:, hidden:].astype(jnp.float32)
    out_ref[other_at, :] = other_ref[:, hidden:].astype(jnp.float32)


def unfold(half, own, other, hidden):
    rows, cols = own.shape
    vmem = pl.BlockSpec(memory_space=pltpu.VMEM)
    return pl.pallas_call(
        unfold_kernel,
        out_shape=(
            jax.ShapeDtypeStruct((2 * rows, hidden), jnp.float32),
            jax.ShapeDtypeStruct((2 * rows, cols - hidden), jnp.float32),
        ),
        in_specs=[pl.BlockSpec(memory_space=pltpu.SMEM), vmem, vmem],
        out_specs=(vmem, vmem),
        compiler_params=pltpu.CompilerParams(vmem_limit_bytes=8 * 1024 * 1024),
        name="unfold",
    )(half, own, other)


def reduce_everywhere(half, keep, give, hidden):
    n_rows, n_cols = keep.shape
    lon_count = lax.axis_size("lon")
    lat_count = lax.axis_size("lat")
    swap = [(0, 1), (1, 0)]
    mine = keep.astype(jnp.float32)
    theirs = lax.ppermute(give, "mem", swap)
    pair = (mine + theirs.astype(jnp.float32)).astype(jnp.bfloat16)
    pieces = lax.all_to_all(
        pair.reshape(lon_count, n_rows // lon_count, n_cols), "lon", split_axis=0, concat_axis=0, tiled=True
    )
    part = jnp.sum(pieces.astype(jnp.float32), axis=0).astype(jnp.bfloat16)
    peers = lax.all_to_all(
        jnp.broadcast_to(part[None], (lat_count,) + part.shape), "lat", split_axis=0, concat_axis=0, tiled=True
    )
    total = jnp.sum(peers.astype(jnp.float32), axis=0).astype(jnp.bfloat16)
    own = lax.all_to_all(
        jnp.broadcast_to(total[None], (lon_count,) + total.shape), "lon", split_axis=0, concat_axis=0, tiled=True
    ).reshape(n_rows, n_cols)
    other = lax.ppermute(own, "mem", swap)
    return unfold(half, own, other, hidden)


def per_device(
    measured_inputs,
    target_sector,
    hidden_member_fields,
    analysis_adjoint,
    inner_perceptron_coeffs,
    outer_perceptron_coeffs,
    probe_projector,
    logit_sharpness,
    adjacent_channel_coeffs,
):
    lon_count = lax.axis_size("lon")
    lat_count = lax.axis_size("lat")
    block_count = target_sector.shape[0]
    model_width = hidden_member_fields.shape[3]
    hidden_width = inner_perceptron_coeffs.shape[1]
    cell_rows = hidden_member_fields.shape[1]
    cell_cols = hidden_member_fields.shape[2]
    n_cells = cell_rows * cell_cols
    cap_slots = max(2, 2 * block_count // lon_count)
    send_blocks = pack_blocks(target_sector, measured_inputs, lon_count, cap_slots)
    obs_blocks = lax.all_to_all(send_blocks, "lon", split_axis=0, concat_axis=0, tiled=True)
    cot_padded = extended(analysis_adjoint[0], (("lon", 1), ("lat", 0)), 1)
    lat_index = lax.axis_index("lat")
    row_ids = lax.broadcasted_iota(jnp.int32, (cell_rows + 2, 1, 1), 0)
    outside = ((row_ids == 0) & (lat_index == 0)) | (
        (row_ids == cell_rows + 1) & (lat_index == lat_count - 1)
    )
    keep_rows = jnp.where(outside, 0.0, 1.0)
    hidden_field_adjoint = (
        mix_local(cot_padded, keep_rows, adjacent_channel_coeffs, -1)
        .astype(jnp.bfloat16)
        .reshape(n_cells, model_width)
    )
    grid_point_entries = hidden_member_fields.reshape(n_cells, model_width)
    prepared = prepare_cells(
        grid_point_entries, hidden_field_adjoint, probe_projector, outer_perceptron_coeffs
    )
    table, xt, self_dots = prepared
    norm = jnp.repeat(logit_sharpness / math.sqrt(CHANNELS_PER_ATT), n_cells)[None, :]
    half = lax.axis_index("mem").astype(jnp.int32).reshape(1)
    revised_analysis, keep, give = tile_step(
        half, obs_blocks.reshape((-1,) + obs_blocks.shape[2:]), table, xt, self_dots, norm,
        inner_perceptron_coeffs, outer_perceptron_coeffs, n_cells,
    )
    in_grad, out_grad = reduce_everywhere(half, keep, give, hidden_width)
    state_grid = revised_analysis.reshape(cell_rows, cell_cols, model_width)
    state_padded = extended(state_grid, (("lon", 1), ("lat", 0)), 1)
    analysis = (
        mix_local(state_padded, keep_rows, adjacent_channel_coeffs, 1)
        .astype(jnp.bfloat16)
        .reshape(hidden_member_fields.shape)
    )
    return (analysis, in_grad, out_grad)


def solution(mesh):
    in_specs = (
        P(("lat", "lon", "mem"), None, None),
        P(("lat", "lon", "mem")),
        P("mem", "lat", "lon", None),
        P("mem", "lat", "lon", None),
        P(),
        P(),
        P(),
        P(),
        P(),
    )
    out_specs = (P("mem", "lat", "lon", None), P(), P())

    return jax.shard_map(per_device, mesh=mesh, in_specs=in_specs, out_specs=out_specs, check_vma=False)
```

```python
import math

import jax
import jax.numpy as jnp
from jax import lax
from jax.experimental import pallas as pl
from jax.experimental.pallas import tpu as pltpu
from jax.sharding import PartitionSpec as P


CHANNELS_PER_ATT = 64
GROUPS = 3
LANES = 256
CHUNK_BLOCKS = 8
PIECE_BLOCKS = 8
MARK = 512.0
TABLE_ROWS = 5 * GROUPS * LANES
ROOM = 40


NEIGHBOURS = ((-1, -1), (-1, 0), (-1, 1), (0, -1), (0, 1), (1, -1), (1, 0), (1, 1))


def extended(block, sides, width, edges=None):
    for axis, dim in sides:
        count = lax.axis_size(axis)
        forward = [(i, i + 1) for i in range(count - 1)]
        forward.append((count - 1, 0))
        backward = [(target, source) for source, target in forward]
        if edges is not None and dim == 1:
            low = lax.ppermute(edges[1], axis, forward)[:, None]
            high = lax.ppermute(edges[0], axis, backward)[:, None]
            block = jnp.concatenate([low, block, high], axis=dim)
            continue
        low = lax.ppermute(
            lax.slice_in_dim(block, block.shape[dim] - width, None, axis=dim), axis, forward
        )
        high = lax.ppermute(lax.slice_in_dim(block, 0, width, axis=dim), axis, backward)
        block = jnp.concatenate([low, block, high], axis=dim)
    return block


def mix_local(padded, keep_rows, adjacent_channel_coeffs, direction):
    values = padded.astype(jnp.float32) * keep_rows
    n_rows = padded.shape[0] - 2
    n_cols = padded.shape[1] - 2
    total = values[1 : 1 + n_rows, 1 : 1 + n_cols]
    for offset_idx, (row_step, col_step) in enumerate(NEIGHBOURS):
        row_start = 1 + direction * row_step
        col_start = 1 + direction * col_step
        total = (
            total
            + adjacent_channel_coeffs[offset_idx]
            * values[row_start : row_start + n_rows, col_start : col_start + n_cols]
        )
    return total


def pack_kernel(
    target_ref, blocks_ref, field_ref, send_ref, first_ref, last_ref,
    count_ref, stage_ref, cells_ref, mark_ref, in_sem, out_sem, mark_sem, cell_sem,
):
    n_blocks = blocks_ref.shape[0]
    n_dest = send_ref.shape[0]
    cap = send_ref.shape[1]
    loads = [pltpu.make_async_copy(blocks_ref.at[b], stage_ref.at[b], in_sem.at[b]) for b in range(n_blocks)]
    cells = pltpu.make_async_copy(field_ref, cells_ref, cell_sem)
    cells.start()
    for load in loads:
        load.start()
    mark_ref[...] = jnp.full(mark_ref.shape, MARK, mark_ref.dtype)
    for d in range(n_dest):
        count_ref[d] = 0

    def copy_of(b, dest, slot):
        return pltpu.make_async_copy(stage_ref.at[b], send_ref.at[dest, slot], out_sem.at[b])

    for b in range(n_blocks):
        dest = target_ref[b]
        slot = count_ref[dest]
        count_ref[dest] = slot + 1
        loads[b].wait()
        copy_of(b, dest, slot).start()

    def mark_of(d, slot):
        return pltpu.make_async_copy(
            mark_ref, send_ref.at[d, slot, pl.ds(0, mark_ref.shape[0])], mark_sem.at[d * cap + slot]
        )

    for d in range(n_dest):
        for slot in range(cap):

            @pl.when(count_ref[d] <= slot)
            def _():
                mark_of(d, slot).start()

    cells.wait()
    grid = [cells_ref[row].astype(jnp.float32) for row in range(cells_ref.shape[0])]
    first_ref[...] = jnp.concatenate([row[0:1] for row in grid], axis=0).astype(first_ref.dtype)
    last_ref[...] = jnp.concatenate([row[-1:] for row in grid], axis=0).astype(last_ref.dtype)
    for b in range(n_blocks):
        copy_of(b, 0, 0).wait()
    for d in range(n_dest):
        for slot in range(cap):

            @pl.when(count_ref[d] <= slot)
            def _():
                mark_of(d, slot).wait()


def pack_blocks(target_sector, blocks, field, n_dest, cap):
    n_blocks, block_len, width = blocks.shape
    vmem = pl.BlockSpec(memory_space=pltpu.VMEM)
    return pl.pallas_call(
        pack_kernel,
        out_shape=(
            jax.ShapeDtypeStruct((n_dest, cap, block_len, width), blocks.dtype),
            jax.ShapeDtypeStruct((field.shape[0], field.shape[2]), field.dtype),
            jax.ShapeDtypeStruct((field.shape[0], field.shape[2]), field.dtype),
        ),
        in_specs=[
            pl.BlockSpec(memory_space=pltpu.SMEM),
            pl.BlockSpec(memory_space=pl.ANY),
            pl.BlockSpec(memory_space=pl.ANY),
        ],
        out_specs=(pl.BlockSpec(memory_space=pl.ANY), vmem, vmem),
        scratch_shapes=[
            pltpu.SMEM((n_dest,), jnp.int32),
            pltpu.VMEM(blocks.shape, blocks.dtype),
            pltpu.VMEM(field.shape, field.dtype),
            pltpu.VMEM((16, width), blocks.dtype),
            pltpu.SemaphoreType.DMA((n_blocks,)),
            pltpu.SemaphoreType.DMA((n_blocks,)),
            pltpu.SemaphoreType.DMA((n_dest * cap,)),
            pltpu.SemaphoreType.DMA,
        ],
        name="pack_blocks",
    )(target_sector, blocks, field)


def block_mask():
    rows = lax.broadcasted_iota(jnp.int32, (LANES, LANES), 0) // CHANNELS_PER_ATT
    cols = lax.broadcasted_iota(jnp.int32, (LANES, LANES), 1) // CHANNELS_PER_ATT
    return rows == cols


def spread(values, group, mask):
    part = values[:, group * LANES : (group + 1) * LANES].astype(jnp.float32)
    return jnp.where(mask, jnp.concatenate([part] * (LANES // CHANNELS_PER_ATT), axis=0), 0.0)


def table_rows(kind, j):
    start = {"q": 0, "g": GROUPS, "gq": 2 * GROUPS, "o": 4 * GROUPS}[kind] + (2 * j if kind == "gq" else j)
    return slice(start * LANES, (start + (2 if kind == "gq" else 1)) * LANES)


def cells_kernel(cells_ref, grad_ref, probe_ref, outer_ref, table_hbm, xt_ref, self_ref, table_ref, sem):
    mask = block_mask()
    query = jnp.dot(cells_ref[...], probe_ref[...], preferred_element_type=jnp.float32)
    query = query.astype(jnp.bfloat16).astype(jnp.float32)
    cells = cells_ref[...].astype(jnp.float32)
    grad = grad_ref[...].astype(jnp.float32)
    for j in range(GROUPS):
        q_rows = spread(query, j, mask)
        g_rows = spread(grad, j, mask)
        table_ref[table_rows("gq", j), :] = jnp.concatenate([g_rows, q_rows], axis=0).astype(jnp.bfloat16)
        q_cols = q_rows.T
        g_cols = g_rows.T
        x_cols = spread(cells, j, mask).T
        table_ref[table_rows("q", j), :] = q_cols.astype(jnp.bfloat16)
        table_ref[table_rows("g", j), :] = g_cols.astype(jnp.bfloat16)
        xt_ref[j] = x_cols
        self_ref[0:1, j * LANES : (j + 1) * LANES] = jnp.sum(q_cols * x_cols, axis=0, keepdims=True)
        self_ref[1:2, j * LANES : (j + 1) * LANES] = jnp.sum(g_cols * x_cols, axis=0, keepdims=True)
        table_ref[table_rows("o", j), :] = (
            outer_ref[:, j * LANES : (j + 1) * LANES].astype(jnp.float32).T.astype(jnp.bfloat16)
        )
    copy = pltpu.make_async_copy(table_ref, table_hbm.at[pl.ds(0, table_ref.shape[0])], sem)
    copy.start()
    copy.wait()


def prepare_cells(cells, grad, probe, outer):
    width = cells.shape[1]
    hidden = outer.shape[0]
    vmem = pl.BlockSpec(memory_space=pltpu.VMEM)
    return pl.pallas_call(
        cells_kernel,
        out_shape=(
            jax.ShapeDtypeStruct((TABLE_ROWS * ROOM, hidden), jnp.bfloat16),
            jax.ShapeDtypeStruct((GROUPS, LANES, LANES), jnp.float32),
            jax.ShapeDtypeStruct((2, width), jnp.float32),
        ),
        out_specs=(pl.BlockSpec(memory_space=pl.ANY), vmem, vmem),
        scratch_shapes=[pltpu.VMEM((TABLE_ROWS, hidden), jnp.bfloat16), pltpu.SemaphoreType.DMA],
        compiler_params=pltpu.CompilerParams(vmem_limit_bytes=12 * 1024 * 1024),
        name="prepare_cells",
    )(cells, grad, probe, outer)


def contract_rows(left, right):
    return lax.dot_general(left, right, (((0,), (0,)), ((), ())), preferred_element_type=jnp.float32)


def tile_kernel(
    half_ref, recv_ref, self_ref, norm_ref, inner_ref, outer_ref, table_hbm, xt_ref,
    state_ref, keep_ref, give_ref,
    table_ref,
    x_s, f_s, p_s, d_s, h_s, m_s, l_s, peak_s, up_s, row_s, in_s, out_s, order_s, live_v, live_s, sem,
):
    n_slots, block_len, _ = recv_ref.shape
    rows = CHUNK_BLOCKS * block_len
    f32 = jnp.float32
    bf16 = jnp.bfloat16

    early = GROUPS * LANES
    early_rows = pl.ds(0, early)
    late_rows = pl.ds(early, TABLE_ROWS - early)
    early_copy = pltpu.make_async_copy(table_hbm.at[early_rows], table_ref.at[early_rows], sem.at[1])
    late_copy = pltpu.make_async_copy(table_hbm.at[late_rows], table_ref.at[late_rows], sem.at[2])
    early_copy.start()
    late_copy.start()
    for i in range(n_slots):
        head = recv_ref[i, 0:16, 0:128].astype(f32)
        live_v[i : i + 1, :] = jnp.where(head[0:1, :] < MARK / 2, 1, 0)
    flags = pltpu.make_async_copy(live_v, live_s, sem.at[0])
    flags.start()
    l_s[...] = jnp.ones_like(l_s)
    up_s[...] = jnp.zeros_like(up_s)
    in_s[...] = jnp.zeros_like(in_s)
    out_s[...] = jnp.zeros_like(out_s)
    flags.wait()
    count = jnp.int32(0)
    for i in range(n_slots):
        order_s[count] = i
        count = count + live_s[i, 0]
    early_copy.wait()
    n_chunks = (count + CHUNK_BLOCKS - 1) // CHUNK_BLOCKS

    norm = norm_ref[...]
    self_score = self_ref[0:1, :] * norm
    m_s[...] = self_score

    def forward(k, carry):
        for i in range(CHUNK_BLOCKS):
            at = k * CHUNK_BLOCKS + i
            at_row = pl.ds(pl.multiple_of(at * block_len, block_len), block_len)

            @pl.when(at < count)
            def _():
                x_s[at_row, :] = recv_ref[order_s[at]]

            @pl.when(at >= count)
            def _():
                x_s[at_row, :] = jnp.zeros((block_len, x_s.shape[1]), bf16)

        start = pl.multiple_of(k * rows, rows)
        piece = PIECE_BLOCKS * block_len
        n_pieces = CHUNK_BLOCKS // PIECE_BLOCKS
        at = [pl.ds(start + i * piece, piece) for i in range(n_pieces)]
        columns = [slice(j * LANES, (j + 1) * LANES) for j in range(GROUPS)]
        bias = [jnp.where(k * CHUNK_BLOCKS + i < count, 0.0, -jnp.inf) for i in range(CHUNK_BLOCKS)]
        for i in range(n_pieces):
            pre = jnp.dot(x_s[at[i], :], inner_ref[...], preferred_element_type=f32)
            gate = 1.0 / (1.0 + jnp.exp(-pre))
            hidden = (pre * gate).astype(bf16)
            d_s[at[i], :] = gate * (1.0 + pre * (1.0 - gate))
            h_s[at[i], :] = hidden
            f_s[at[i], :] = jnp.dot(hidden, outer_ref[...], preferred_element_type=f32).astype(bf16)

        def score(j, i):
            raw = jnp.dot(f_s[at[i], columns[j]], table_ref[table_rows("q", j), :], preferred_element_type=f32)
            raw = raw * norm[:, columns[j]]
            top = None
            for n in range(PIECE_BLOCKS):
                part = raw[n * block_len : (n + 1) * block_len] + bias[i * PIECE_BLOCKS + n]
                p_s[pl.ds(start + i * piece + n * block_len, block_len), columns[j]] = part
                part_top = jnp.max(part, axis=0, keepdims=True)
                top = part_top if top is None else jnp.maximum(top, part_top)
            return top

        tops = [score(0, i) for i in range(n_pieces)]
        for j in range(GROUPS):
            cols = columns[j]
            old = m_s[:, cols]
            peak = old
            for top in tops:
                peak = jnp.maximum(peak, top)
            fade = jnp.exp(old - peak)
            total = l_s[:, cols] * fade
            update = up_s[j] * fade
            tops = []
            for i in range(n_pieces):
                terms = jnp.exp(p_s[at[i], cols] - peak)
                p_s[at[i], cols] = terms
                total = total + jnp.sum(terms, axis=0, keepdims=True)
                if j + 1 < GROUPS:
                    tops.append(score(j + 1, i))
                update = update + contract_rows(f_s[at[i], cols], terms.astype(bf16))
            m_s[:, cols] = peak
            peak_s[k, :, cols] = peak
            l_s[:, cols] = total
            up_s[j] = update
        return carry

    lax.fori_loop(0, n_chunks, forward, 0)

    late_copy.wait()
    mask = block_mask()
    inverse = 1.0 / l_s[...]
    peak = m_s[...]
    self_prob = jnp.exp(self_score - peak) * inverse
    self_weight = self_prob.astype(bf16).astype(f32)
    for j in range(GROUPS):
        cols = slice(j * LANES, (j + 1) * LANES)
        update = jnp.where(mask, up_s[j] * inverse[:, cols], 0.0)
        row_s[:, cols] = (
            jnp.sum(update * table_ref[table_rows("g", j), :].astype(f32), axis=0, keepdims=True)
            + self_prob[:, cols] * self_ref[1:2, cols]
        )
        x_cols = xt_ref[j]
        state = (x_cols + (update + self_weight[:, cols] * x_cols)).T
        total = state[0:CHANNELS_PER_ATT]
        for h in range(1, LANES // CHANNELS_PER_ATT):
            total = total + state[h * CHANNELS_PER_ATT : (h + 1) * CHANNELS_PER_ATT]
        state_ref[:, cols] = total.astype(bf16)

    row_total = row_s[...]

    def backward(k, carry):
        start = pl.multiple_of(k * rows, rows)
        here = pl.ds(start, rows)
        scale = jnp.exp(peak_s[k] - peak) * inverse
        scaled = scale * norm
        hidden = h_s[here, :]
        hidden_grad = jnp.zeros((rows, LANES), f32)
        for j in range(GROUPS):
            cols = slice(j * LANES, (j + 1) * LANES)
            terms = p_s[here, cols]
            weights = (terms * scale[:, cols]).astype(bf16)
            weight_grad = jnp.dot(
                f_s[here, cols], table_ref[table_rows("g", j), :], preferred_element_type=f32
            )
            logit_grad = ((terms * scaled[:, cols]) * (weight_grad - row_total[:, cols])).astype(bf16)
            feat_grad = jnp.dot(
                jnp.concatenate([weights, logit_grad], axis=1),
                table_ref[table_rows("gq", j), :],
                preferred_element_type=f32,
            ).astype(bf16)
            hidden_grad = hidden_grad + jnp.dot(
                feat_grad, table_ref[table_rows("o", j), :], preferred_element_type=f32
            )
            out_s[:, cols] = out_s[:, cols] + contract_rows(hidden, feat_grad)
        hidden_grad = (hidden_grad * d_s[here, :]).astype(bf16)
        in_s[...] = in_s[...] + contract_rows(x_s[here, :], hidden_grad)
        return carry

    lax.fori_loop(0, n_chunks, backward, 0)
    n_rows = keep_ref.shape[0]
    split = in_s.shape[1]
    for dst, half in ((keep_ref, half_ref[0]), (give_ref, 1 - half_ref[0])):
        here = pl.ds(pl.multiple_of(half * n_rows, n_rows), n_rows)
        dst[:, 0:split] = in_s[here, :].astype(bf16)
        dst[:, split:] = out_s[here, :].astype(bf16)


def tile_step(half, recv, table, xt, self_dots, norm, inner, outer, n_cells):
    n_slots, block_len, obs_width = recv.shape
    hidden, width = outer.shape
    n_tokens = n_slots * block_len
    n_chunks = n_slots // CHUNK_BLOCKS
    vmem = pl.BlockSpec(memory_space=pltpu.VMEM)
    return pl.pallas_call(
        tile_kernel,
        out_shape=(
            jax.ShapeDtypeStruct((n_cells, width), jnp.bfloat16),
            jax.ShapeDtypeStruct((obs_width // 2, hidden + width), jnp.bfloat16),
            jax.ShapeDtypeStruct((obs_width // 2, hidden + width), jnp.bfloat16),
        ),
        in_specs=[pl.BlockSpec(memory_space=pltpu.SMEM)]
        + [vmem] * 5
        + [pl.BlockSpec(memory_space=pl.ANY), vmem],
        out_specs=(vmem, vmem, vmem),
        scratch_shapes=[
            pltpu.VMEM((TABLE_ROWS, hidden), table.dtype),
            pltpu.VMEM((n_tokens, obs_width), jnp.bfloat16),
            pltpu.VMEM((n_tokens, width), jnp.bfloat16),
            pltpu.VMEM((n_tokens, width), jnp.float32),
            pltpu.VMEM((n_tokens, hidden), jnp.float32),
            pltpu.VMEM((n_tokens, hidden), jnp.bfloat16),
            pltpu.VMEM((1, width), jnp.float32),
            pltpu.VMEM((1, width), jnp.float32),
            pltpu.VMEM((n_chunks, 1, width), jnp.float32),
            pltpu.VMEM((GROUPS, LANES, LANES), jnp.float32),
            pltpu.VMEM((1, width), jnp.float32),
            pltpu.VMEM((obs_width, hidden), jnp.float32),
            pltpu.VMEM((hidden, width), jnp.float32),
            pltpu.SMEM((n_slots + 1,), jnp.int32),
            pltpu.VMEM((n_slots, 128), jnp.int32),
            pltpu.SMEM((n_slots, 128), jnp.int32),
            pltpu.SemaphoreType.DMA((3,)),
        ],
        compiler_params=pltpu.CompilerParams(vmem_limit_bytes=44 * 1024 * 1024),
        name="tile_step",
    )(half, recv, self_dots, norm, inner, outer, table, xt)


def unfold_kernel(half_ref, own_ref, other_ref, in_ref, out_ref):
    rows, _ = own_ref.shape
    hidden = in_ref.shape[1]
    own_at = pl.ds(pl.multiple_of(half_ref[0] * rows, rows), rows)
    other_at = pl.ds(pl.multiple_of((1 - half_ref[0]) * rows, rows), rows)
    in_ref[own_at, :] = own_ref[:, 0:hidden].astype(jnp.float32)
    in_ref[other_at, :] = other_ref[:, 0:hidden].astype(jnp.float32)
    out_ref[own_at, :] = own_ref[:, hidden:].astype(jnp.float32)
    out_ref[other_at, :] = other_ref[:, hidden:].astype(jnp.float32)


def unfold(half, own, other, hidden):
    rows, cols = own.shape
    vmem = pl.BlockSpec(memory_space=pltpu.VMEM)
    return pl.pallas_call(
        unfold_kernel,
        out_shape=(
            jax.ShapeDtypeStruct((2 * rows, hidden), jnp.float32),
            jax.ShapeDtypeStruct((2 * rows, cols - hidden), jnp.float32),
        ),
        in_specs=[pl.BlockSpec(memory_space=pltpu.SMEM), vmem, vmem],
        out_specs=(vmem, vmem),
        compiler_params=pltpu.CompilerParams(vmem_limit_bytes=8 * 1024 * 1024),
        name="unfold",
    )(half, own, other)


def reduce_everywhere(half, keep, give, hidden):
    n_rows, n_cols = keep.shape
    lon_count = lax.axis_size("lon")
    lat_count = lax.axis_size("lat")
    swap = [(0, 1), (1, 0)]
    mine = keep.astype(jnp.float32)
    theirs = lax.ppermute(give, "mem", swap)
    pair = (mine + theirs.astype(jnp.float32)).astype(jnp.bfloat16)
    pieces = lax.all_to_all(
        pair.reshape(lon_count, n_rows // lon_count, n_cols), "lon", split_axis=0, concat_axis=0, tiled=True
    )
    part = jnp.sum(pieces.astype(jnp.float32), axis=0).astype(jnp.bfloat16)
    peers = lax.all_to_all(
        jnp.broadcast_to(part[None], (lat_count,) + part.shape), "lat", split_axis=0, concat_axis=0, tiled=True
    )
    total = jnp.sum(peers.astype(jnp.float32), axis=0).astype(jnp.bfloat16)
    own = lax.all_to_all(
        jnp.broadcast_to(total[None], (lon_count,) + total.shape), "lon", split_axis=0, concat_axis=0, tiled=True
    ).reshape(n_rows, n_cols)
    other = lax.ppermute(own, "mem", swap)
    return unfold(half, own, other, hidden)


def per_device(
    measured_inputs,
    target_sector,
    hidden_member_fields,
    analysis_adjoint,
    inner_perceptron_coeffs,
    outer_perceptron_coeffs,
    probe_projector,
    logit_sharpness,
    adjacent_channel_coeffs,
):
    lon_count = lax.axis_size("lon")
    lat_count = lax.axis_size("lat")
    block_count = target_sector.shape[0]
    model_width = hidden_member_fields.shape[3]
    hidden_width = inner_perceptron_coeffs.shape[1]
    cell_rows = hidden_member_fields.shape[1]
    cell_cols = hidden_member_fields.shape[2]
    n_cells = cell_rows * cell_cols
    cap_slots = max(2, 2 * block_count // lon_count)
    send_blocks, first_edge, last_edge = pack_blocks(
        target_sector, measured_inputs, analysis_adjoint[0], lon_count, cap_slots
    )
    obs_blocks = lax.all_to_all(send_blocks, "lon", split_axis=0, concat_axis=0, tiled=True)
    cot_padded = extended(analysis_adjoint[0], (("lon", 1), ("lat", 0)), 1, (first_edge, last_edge))
    lat_index = lax.axis_index("lat")
    row_ids = lax.broadcasted_iota(jnp.int32, (cell_rows + 2, 1, 1), 0)
    outside = ((row_ids == 0) & (lat_index == 0)) | (
        (row_ids == cell_rows + 1) & (lat_index == lat_count - 1)
    )
    keep_rows = jnp.where(outside, 0.0, 1.0)
    hidden_field_adjoint = (
        mix_local(cot_padded, keep_rows, adjacent_channel_coeffs, -1)
        .astype(jnp.bfloat16)
        .reshape(n_cells, model_width)
    )
    grid_point_entries = hidden_member_fields.reshape(n_cells, model_width)
    prepared = prepare_cells(
        grid_point_entries, hidden_field_adjoint, probe_projector, outer_perceptron_coeffs
    )
    table, xt, self_dots = prepared
    norm = jnp.repeat(logit_sharpness / math.sqrt(CHANNELS_PER_ATT), n_cells)[None, :]
    half = lax.axis_index("mem").astype(jnp.int32).reshape(1)
    revised_analysis, keep, give = tile_step(
        half, obs_blocks.reshape((-1,) + obs_blocks.shape[2:]), table, xt, self_dots, norm,
        inner_perceptron_coeffs, outer_perceptron_coeffs, n_cells,
    )
    in_grad, out_grad = reduce_everywhere(half, keep, give, hidden_width)
    state_grid = revised_analysis.reshape(cell_rows, cell_cols, model_width)
    state_padded = extended(state_grid, (("lon", 1), ("lat", 0)), 1)
    analysis = (
        mix_local(state_padded, keep_rows, adjacent_channel_coeffs, 1)
        .astype(jnp.bfloat16)
        .reshape(hidden_member_fields.shape)
    )
    return (analysis, in_grad, out_grad)


def solution(mesh):
    in_specs = (
        P(("lat", "lon", "mem"), None, None),
        P(("lat", "lon", "mem")),
        P("mem", "lat", "lon", None),
        P("mem", "lat", "lon", None),
        P(),
        P(),
        P(),
        P(),
        P(),
    )
    out_specs = (P("mem", "lat", "lon", None), P(), P())

    return jax.shard_map(per_device, mesh=mesh, in_specs=in_specs, out_specs=out_specs, check_vma=False)
```

```python
import math

import jax
import jax.numpy as jnp
from jax import lax
from jax.experimental import pallas as pl
from jax.experimental.pallas import tpu as pltpu
from jax.sharding import PartitionSpec as P


CHANNELS_PER_ATT = 64
GROUPS = 3
LANES = 256
CHUNK_BLOCKS = 16
PIECE_BLOCKS = 8
MARK = 512.0
TABLE_ROWS = 5 * GROUPS * LANES
ROOM = 40


NEIGHBOURS = ((-1, -1), (-1, 0), (-1, 1), (0, -1), (0, 1), (1, -1), (1, 0), (1, 1))


def extended(block, sides, width, edges=None):
    for axis, dim in sides:
        count = lax.axis_size(axis)
        forward = [(i, i + 1) for i in range(count - 1)]
        forward.append((count - 1, 0))
        backward = [(target, source) for source, target in forward]
        if edges is not None and dim == 1:
            low = lax.ppermute(edges[1], axis, forward)[:, None]
            high = lax.ppermute(edges[0], axis, backward)[:, None]
            block = jnp.concatenate([low, block, high], axis=dim)
            continue
        low = lax.ppermute(
            lax.slice_in_dim(block, block.shape[dim] - width, None, axis=dim), axis, forward
        )
        high = lax.ppermute(lax.slice_in_dim(block, 0, width, axis=dim), axis, backward)
        block = jnp.concatenate([low, block, high], axis=dim)
    return block


def mix_local(padded, keep_rows, adjacent_channel_coeffs, direction):
    values = padded.astype(jnp.float32) * keep_rows
    n_rows = padded.shape[0] - 2
    n_cols = padded.shape[1] - 2
    total = values[1 : 1 + n_rows, 1 : 1 + n_cols]
    for offset_idx, (row_step, col_step) in enumerate(NEIGHBOURS):
        row_start = 1 + direction * row_step
        col_start = 1 + direction * col_step
        total = (
            total
            + adjacent_channel_coeffs[offset_idx]
            * values[row_start : row_start + n_rows, col_start : col_start + n_cols]
        )
    return total


def pack_kernel(
    target_ref, blocks_ref, field_ref, send_ref, first_ref, last_ref,
    count_ref, stage_ref, cells_ref, mark_ref, in_sem, out_sem, mark_sem, cell_sem,
):
    n_blocks = blocks_ref.shape[0]
    n_dest = send_ref.shape[0]
    cap = send_ref.shape[1]
    loads = [pltpu.make_async_copy(blocks_ref.at[b], stage_ref.at[b], in_sem.at[b]) for b in range(n_blocks)]
    cells = pltpu.make_async_copy(field_ref, cells_ref, cell_sem)
    cells.start()
    for load in loads:
        load.start()
    mark_ref[...] = jnp.full(mark_ref.shape, MARK, mark_ref.dtype)
    for d in range(n_dest):
        count_ref[d] = 0

    def copy_of(b, dest, slot):
        return pltpu.make_async_copy(stage_ref.at[b], send_ref.at[dest, slot], out_sem.at[b])

    places = []
    for b in range(n_blocks):
        dest = target_ref[b]
        slot = count_ref[dest]
        count_ref[dest] = slot + 1
        places.append((dest, slot))

    def mark_of(d, slot):
        return pltpu.make_async_copy(
            mark_ref, send_ref.at[d, slot, pl.ds(0, mark_ref.shape[0])], mark_sem.at[d * cap + slot]
        )

    for d in range(n_dest):
        for slot in range(cap):

            @pl.when(count_ref[d] <= slot)
            def _():
                mark_of(d, slot).start()

    for b, (dest, slot) in enumerate(places):
        loads[b].wait()
        copy_of(b, dest, slot).start()
    cells.wait()
    grid = [cells_ref[row].astype(jnp.float32) for row in range(cells_ref.shape[0])]
    first_ref[...] = jnp.concatenate([row[0:1] for row in grid], axis=0).astype(first_ref.dtype)
    last_ref[...] = jnp.concatenate([row[-1:] for row in grid], axis=0).astype(last_ref.dtype)
    for b in range(n_blocks):
        copy_of(b, 0, 0).wait()
    for d in range(n_dest):
        for slot in range(cap):

            @pl.when(count_ref[d] <= slot)
            def _():
                mark_of(d, slot).wait()


def pack_blocks(target_sector, blocks, field, n_dest, cap):
    n_blocks, block_len, width = blocks.shape
    vmem = pl.BlockSpec(memory_space=pltpu.VMEM)
    return pl.pallas_call(
        pack_kernel,
        out_shape=(
            jax.ShapeDtypeStruct((n_dest, cap, block_len, width), blocks.dtype),
            jax.ShapeDtypeStruct((field.shape[0], field.shape[2]), field.dtype),
            jax.ShapeDtypeStruct((field.shape[0], field.shape[2]), field.dtype),
        ),
        in_specs=[
            pl.BlockSpec(memory_space=pltpu.SMEM),
            pl.BlockSpec(memory_space=pl.ANY),
            pl.BlockSpec(memory_space=pl.ANY),
        ],
        out_specs=(pl.BlockSpec(memory_space=pl.ANY), vmem, vmem),
        scratch_shapes=[
            pltpu.SMEM((n_dest,), jnp.int32),
            pltpu.VMEM(blocks.shape, blocks.dtype),
            pltpu.VMEM(field.shape, field.dtype),
            pltpu.VMEM((16, width), blocks.dtype),
            pltpu.SemaphoreType.DMA((n_blocks,)),
            pltpu.SemaphoreType.DMA((n_blocks,)),
            pltpu.SemaphoreType.DMA((n_dest * cap,)),
            pltpu.SemaphoreType.DMA,
        ],
        name="pack_blocks",
    )(target_sector, blocks, field)


def block_mask():
    rows = lax.broadcasted_iota(jnp.int32, (LANES, LANES), 0) // CHANNELS_PER_ATT
    cols = lax.broadcasted_iota(jnp.int32, (LANES, LANES), 1) // CHANNELS_PER_ATT
    return rows == cols


def spread(values, group, mask):
    part = values[:, group * LANES : (group + 1) * LANES].astype(jnp.float32)
    return jnp.where(mask, jnp.concatenate([part] * (LANES // CHANNELS_PER_ATT), axis=0), 0.0)


def table_rows(kind, j):
    start = {"q": 0, "g": GROUPS, "gq": 2 * GROUPS, "o": 4 * GROUPS}[kind] + (2 * j if kind == "gq" else j)
    return slice(start * LANES, (start + (2 if kind == "gq" else 1)) * LANES)


def cells_kernel(cells_ref, grad_ref, probe_ref, outer_ref, table_hbm, xt_ref, self_ref, table_ref, sem):
    mask = block_mask()
    query = jnp.dot(cells_ref[...], probe_ref[...], preferred_element_type=jnp.float32)
    query = query.astype(jnp.bfloat16).astype(jnp.float32)
    cells = cells_ref[...].astype(jnp.float32)
    grad = grad_ref[...].astype(jnp.float32)
    for j in range(GROUPS):
        q_rows = spread(query, j, mask)
        g_rows = spread(grad, j, mask)
        table_ref[table_rows("gq", j), :] = jnp.concatenate([g_rows, q_rows], axis=0).astype(jnp.bfloat16)
        q_cols = q_rows.T
        g_cols = g_rows.T
        x_cols = spread(cells, j, mask).T
        table_ref[table_rows("q", j), :] = q_cols.astype(jnp.bfloat16)
        table_ref[table_rows("g", j), :] = g_cols.astype(jnp.bfloat16)
        xt_ref[j] = x_cols
        self_ref[0:1, j * LANES : (j + 1) * LANES] = jnp.sum(q_cols * x_cols, axis=0, keepdims=True)
        self_ref[1:2, j * LANES : (j + 1) * LANES] = jnp.sum(g_cols * x_cols, axis=0, keepdims=True)
        table_ref[table_rows("o", j), :] = (
            outer_ref[:, j * LANES : (j + 1) * LANES].astype(jnp.float32).T.astype(jnp.bfloat16)
        )
    copy = pltpu.make_async_copy(table_ref, table_hbm.at[pl.ds(0, table_ref.shape[0])], sem)
    copy.start()
    copy.wait()


def prepare_cells(cells, grad, probe, outer):
    width = cells.shape[1]
    hidden = outer.shape[0]
    vmem = pl.BlockSpec(memory_space=pltpu.VMEM)
    return pl.pallas_call(
        cells_kernel,
        out_shape=(
            jax.ShapeDtypeStruct((TABLE_ROWS * ROOM, hidden), jnp.bfloat16),
            jax.ShapeDtypeStruct((GROUPS, LANES, LANES), jnp.float32),
            jax.ShapeDtypeStruct((2, width), jnp.float32),
        ),
        out_specs=(pl.BlockSpec(memory_space=pl.ANY), vmem, vmem),
        scratch_shapes=[pltpu.VMEM((TABLE_ROWS, hidden), jnp.bfloat16), pltpu.SemaphoreType.DMA],
        compiler_params=pltpu.CompilerParams(vmem_limit_bytes=12 * 1024 * 1024),
        name="prepare_cells",
    )(cells, grad, probe, outer)


def contract_rows(left, right):
    return lax.dot_general(left, right, (((0,), (0,)), ((), ())), preferred_element_type=jnp.float32)


def tile_kernel(
    half_ref, recv_ref, self_ref, norm_ref, inner_ref, outer_ref, table_hbm, xt_ref,
    state_ref, keep_ref, give_ref,
    table_ref,
    x_s, f_s, p_s, d_s, h_s, m_s, l_s, peak_s, up_s, row_s, in_s, out_s, order_s, live_v, live_s, sem,
):
    n_slots, block_len, _ = recv_ref.shape
    rows = CHUNK_BLOCKS * block_len
    f32 = jnp.float32
    bf16 = jnp.bfloat16

    early = GROUPS * LANES
    early_rows = pl.ds(0, early)
    late_rows = pl.ds(early, TABLE_ROWS - early)
    early_copy = pltpu.make_async_copy(table_hbm.at[early_rows], table_ref.at[early_rows], sem.at[1])
    late_copy = pltpu.make_async_copy(table_hbm.at[late_rows], table_ref.at[late_rows], sem.at[2])
    early_copy.start()
    late_copy.start()
    for i in range(n_slots):
        head = recv_ref[i, 0:16, 0:128].astype(f32)
        live_v[i : i + 1, :] = jnp.where(head[0:1, :] < MARK / 2, 1, 0)
    flags = pltpu.make_async_copy(live_v, live_s, sem.at[0])
    flags.start()
    l_s[...] = jnp.ones_like(l_s)
    up_s[...] = jnp.zeros_like(up_s)
    in_s[...] = jnp.zeros_like(in_s)
    out_s[...] = jnp.zeros_like(out_s)
    flags.wait()
    count = jnp.int32(0)
    for i in range(n_slots):
        order_s[count] = i
        count = count + live_s[i, 0]
    early_copy.wait()
    n_chunks = (count + CHUNK_BLOCKS - 1) // CHUNK_BLOCKS

    norm = norm_ref[...]
    self_score = self_ref[0:1, :] * norm
    m_s[...] = self_score

    def forward(k, carry):
        for i in range(CHUNK_BLOCKS):
            at = k * CHUNK_BLOCKS + i
            at_row = pl.ds(pl.multiple_of(at * block_len, block_len), block_len)

            @pl.when(at < count)
            def _():
                x_s[at_row, :] = recv_ref[order_s[at]]

            @pl.when(at >= count)
            def _():
                x_s[at_row, :] = jnp.zeros((block_len, x_s.shape[1]), bf16)

        start = pl.multiple_of(k * rows, rows)
        piece = PIECE_BLOCKS * block_len
        n_pieces = CHUNK_BLOCKS // PIECE_BLOCKS
        at = [pl.ds(start + i * piece, piece) for i in range(n_pieces)]
        columns = [slice(j * LANES, (j + 1) * LANES) for j in range(GROUPS)]
        bias = [jnp.where(k * CHUNK_BLOCKS + i < count, 0.0, -jnp.inf) for i in range(CHUNK_BLOCKS)]
        for i in range(n_pieces):
            pre = jnp.dot(x_s[at[i], :], inner_ref[...], preferred_element_type=f32)
            gate = 1.0 / (1.0 + jnp.exp(-pre))
            hidden = (pre * gate).astype(bf16)
            d_s[at[i], :] = gate * (1.0 + pre * (1.0 - gate))
            h_s[at[i], :] = hidden
            f_s[at[i], :] = jnp.dot(hidden, outer_ref[...], preferred_element_type=f32).astype(bf16)

        def score(j, i):
            raw = jnp.dot(f_s[at[i], columns[j]], table_ref[table_rows("q", j), :], preferred_element_type=f32)
            raw = raw * norm[:, columns[j]]
            top = None
            for n in range(PIECE_BLOCKS):
                part = raw[n * block_len : (n + 1) * block_len] + bias[i * PIECE_BLOCKS + n]
                p_s[pl.ds(start + i * piece + n * block_len, block_len), columns[j]] = part
                part_top = jnp.max(part, axis=0, keepdims=True)
                top = part_top if top is None else jnp.maximum(top, part_top)
            return top

        tops = [score(0, i) for i in range(n_pieces)]
        for j in range(GROUPS):
            cols = columns[j]
            old = m_s[:, cols]
            peak = old
            for top in tops:
                peak = jnp.maximum(peak, top)
            fade = jnp.exp(old - peak)
            total = l_s[:, cols] * fade
            update = up_s[j] * fade
            tops = []
            for i in range(n_pieces):
                terms = jnp.exp(p_s[at[i], cols] - peak)
                p_s[at[i], cols] = terms
                total = total + jnp.sum(terms, axis=0, keepdims=True)
                if j + 1 < GROUPS:
                    tops.append(score(j + 1, i))
                update = update + contract_rows(f_s[at[i], cols], terms.astype(bf16))
            m_s[:, cols] = peak
            peak_s[k, :, cols] = peak
            l_s[:, cols] = total
            up_s[j] = update
        return carry

    lax.fori_loop(0, n_chunks, forward, 0)

    late_copy.wait()
    mask = block_mask()
    inverse = 1.0 / l_s[...]
    peak = m_s[...]
    self_prob = jnp.exp(self_score - peak) * inverse
    self_weight = self_prob.astype(bf16).astype(f32)
    for j in range(GROUPS):
        cols = slice(j * LANES, (j + 1) * LANES)
        update = jnp.where(mask, up_s[j] * inverse[:, cols], 0.0)
        row_s[:, cols] = (
            jnp.sum(update * table_ref[table_rows("g", j), :].astype(f32), axis=0, keepdims=True)
            + self_prob[:, cols] * self_ref[1:2, cols]
        )
        x_cols = xt_ref[j]
        state = (x_cols + (update + self_weight[:, cols] * x_cols)).T
        total = state[0:CHANNELS_PER_ATT]
        for h in range(1, LANES // CHANNELS_PER_ATT):
            total = total + state[h * CHANNELS_PER_ATT : (h + 1) * CHANNELS_PER_ATT]
        state_ref[:, cols] = total.astype(bf16)

    row_total = row_s[...]

    def backward(k, carry):
        start = pl.multiple_of(k * rows, rows)
        here = pl.ds(start, rows)
        scale = jnp.exp(peak_s[k] - peak) * inverse
        scaled = scale * norm
        hidden = h_s[here, :]
        hidden_grad = jnp.zeros((rows, LANES), f32)
        for j in range(GROUPS):
            cols = slice(j * LANES, (j + 1) * LANES)
            terms = p_s[here, cols]
            weights = (terms * scale[:, cols]).astype(bf16)
            weight_grad = jnp.dot(
                f_s[here, cols], table_ref[table_rows("g", j), :], preferred_element_type=f32
            )
            logit_grad = ((terms * scaled[:, cols]) * (weight_grad - row_total[:, cols])).astype(bf16)
            feat_grad = jnp.dot(
                jnp.concatenate([weights, logit_grad], axis=1),
                table_ref[table_rows("gq", j), :],
                preferred_element_type=f32,
            ).astype(bf16)
            hidden_grad = hidden_grad + jnp.dot(
                feat_grad, table_ref[table_rows("o", j), :], preferred_element_type=f32
            )
            out_s[:, cols] = out_s[:, cols] + contract_rows(hidden, feat_grad)
        hidden_grad = (hidden_grad * d_s[here, :]).astype(bf16)
        in_s[...] = in_s[...] + contract_rows(x_s[here, :], hidden_grad)
        return carry

    lax.fori_loop(0, n_chunks, backward, 0)
    n_rows = keep_ref.shape[0]
    split = in_s.shape[1]
    for dst, half in ((keep_ref, half_ref[0]), (give_ref, 1 - half_ref[0])):
        here = pl.ds(pl.multiple_of(half * n_rows, n_rows), n_rows)
        dst[:, 0:split] = in_s[here, :].astype(bf16)
        dst[:, split:] = out_s[here, :].astype(bf16)


def tile_step(half, recv, table, xt, self_dots, norm, inner, outer, n_cells):
    n_slots, block_len, obs_width = recv.shape
    hidden, width = outer.shape
    n_tokens = n_slots * block_len
    n_chunks = n_slots // CHUNK_BLOCKS
    vmem = pl.BlockSpec(memory_space=pltpu.VMEM)
    return pl.pallas_call(
        tile_kernel,
        out_shape=(
            jax.ShapeDtypeStruct((n_cells, width), jnp.bfloat16),
            jax.ShapeDtypeStruct((obs_width // 2, hidden + width), jnp.bfloat16),
            jax.ShapeDtypeStruct((obs_width // 2, hidden + width), jnp.bfloat16),
        ),
        in_specs=[pl.BlockSpec(memory_space=pltpu.SMEM)]
        + [vmem] * 5
        + [pl.BlockSpec(memory_space=pl.ANY), vmem],
        out_specs=(vmem, vmem, vmem),
        scratch_shapes=[
            pltpu.VMEM((TABLE_ROWS, hidden), table.dtype),
            pltpu.VMEM((n_tokens, obs_width), jnp.bfloat16),
            pltpu.VMEM((n_tokens, width), jnp.bfloat16),
            pltpu.VMEM((n_tokens, width), jnp.float32),
            pltpu.VMEM((n_tokens, hidden), jnp.float32),
            pltpu.VMEM((n_tokens, hidden), jnp.bfloat16),
            pltpu.VMEM((1, width), jnp.float32),
            pltpu.VMEM((1, width), jnp.float32),
            pltpu.VMEM((n_chunks, 1, width), jnp.float32),
            pltpu.VMEM((GROUPS, LANES, LANES), jnp.float32),
            pltpu.VMEM((1, width), jnp.float32),
            pltpu.VMEM((obs_width, hidden), jnp.float32),
            pltpu.VMEM((hidden, width), jnp.float32),
            pltpu.SMEM((n_slots + 1,), jnp.int32),
            pltpu.VMEM((n_slots, 128), jnp.int32),
            pltpu.SMEM((n_slots, 128), jnp.int32),
            pltpu.SemaphoreType.DMA((3,)),
        ],
        compiler_params=pltpu.CompilerParams(vmem_limit_bytes=44 * 1024 * 1024),
        name="tile_step",
    )(half, recv, self_dots, norm, inner, outer, table, xt)


def unfold_kernel(half_ref, own_ref, other_ref, in_ref, out_ref):
    rows, _ = own_ref.shape
    hidden = in_ref.shape[1]
    own_at = pl.ds(pl.multiple_of(half_ref[0] * rows, rows), rows)
    other_at = pl.ds(pl.multiple_of((1 - half_ref[0]) * rows, rows), rows)
    in_ref[own_at, :] = own_ref[:, 0:hidden].astype(jnp.float32)
    in_ref[other_at, :] = other_ref[:, 0:hidden].astype(jnp.float32)
    out_ref[own_at, :] = own_ref[:, hidden:].astype(jnp.float32)
    out_ref[other_at, :] = other_ref[:, hidden:].astype(jnp.float32)


def unfold(half, own, other, hidden):
    rows, cols = own.shape
    vmem = pl.BlockSpec(memory_space=pltpu.VMEM)
    return pl.pallas_call(
        unfold_kernel,
        out_shape=(
            jax.ShapeDtypeStruct((2 * rows, hidden), jnp.float32),
            jax.ShapeDtypeStruct((2 * rows, cols - hidden), jnp.float32),
        ),
        in_specs=[pl.BlockSpec(memory_space=pltpu.SMEM), vmem, vmem],
        out_specs=(vmem, vmem),
        compiler_params=pltpu.CompilerParams(vmem_limit_bytes=8 * 1024 * 1024),
        name="unfold",
    )(half, own, other)


def reduce_everywhere(half, keep, give, hidden):
    n_rows, n_cols = keep.shape
    lon_count = lax.axis_size("lon")
    lat_count = lax.axis_size("lat")
    swap = [(0, 1), (1, 0)]
    mine = keep.astype(jnp.float32)
    theirs = lax.ppermute(give, "mem", swap)
    pair = (mine + theirs.astype(jnp.float32)).astype(jnp.bfloat16)
    pieces = lax.all_to_all(
        pair.reshape(lon_count, n_rows // lon_count, n_cols), "lon", split_axis=0, concat_axis=0, tiled=True
    )
    part = jnp.sum(pieces.astype(jnp.float32), axis=0).astype(jnp.bfloat16)
    peers = lax.all_to_all(
        jnp.broadcast_to(part[None], (lat_count,) + part.shape), "lat", split_axis=0, concat_axis=0, tiled=True
    )
    total = jnp.sum(peers.astype(jnp.float32), axis=0).astype(jnp.bfloat16)
    own = lax.all_to_all(
        jnp.broadcast_to(total[None], (lon_count,) + total.shape), "lon", split_axis=0, concat_axis=0, tiled=True
    ).reshape(n_rows, n_cols)
    other = lax.ppermute(own, "mem", swap)
    return unfold(half, own, other, hidden)


def per_device(
    measured_inputs,
    target_sector,
    hidden_member_fields,
    analysis_adjoint,
    inner_perceptron_coeffs,
    outer_perceptron_coeffs,
    probe_projector,
    logit_sharpness,
    adjacent_channel_coeffs,
):
    lon_count = lax.axis_size("lon")
    lat_count = lax.axis_size("lat")
    block_count = target_sector.shape[0]
    model_width = hidden_member_fields.shape[3]
    hidden_width = inner_perceptron_coeffs.shape[1]
    cell_rows = hidden_member_fields.shape[1]
    cell_cols = hidden_member_fields.shape[2]
    n_cells = cell_rows * cell_cols
    cap_slots = max(2, 2 * block_count // lon_count)
    send_blocks, first_edge, last_edge = pack_blocks(
        target_sector, measured_inputs, analysis_adjoint[0], lon_count, cap_slots
    )
    obs_blocks = lax.all_to_all(send_blocks, "lon", split_axis=0, concat_axis=0, tiled=True)
    cot_padded = extended(analysis_adjoint[0], (("lon", 1), ("lat", 0)), 1, (first_edge, last_edge))
    lat_index = lax.axis_index("lat")
    row_ids = lax.broadcasted_iota(jnp.int32, (cell_rows + 2, 1, 1), 0)
    outside = ((row_ids == 0) & (lat_index == 0)) | (
        (row_ids == cell_rows + 1) & (lat_index == lat_count - 1)
    )
    keep_rows = jnp.where(outside, 0.0, 1.0)
    hidden_field_adjoint = (
        mix_local(cot_padded, keep_rows, adjacent_channel_coeffs, -1)
        .astype(jnp.bfloat16)
        .reshape(n_cells, model_width)
    )
    grid_point_entries = hidden_member_fields.reshape(n_cells, model_width)
    prepared = prepare_cells(
        grid_point_entries, hidden_field_adjoint, probe_projector, outer_perceptron_coeffs
    )
    table, xt, self_dots = prepared
    norm = jnp.repeat(logit_sharpness / math.sqrt(CHANNELS_PER_ATT), n_cells)[None, :]
    half = lax.axis_index("mem").astype(jnp.int32).reshape(1)
    revised_analysis, keep, give = tile_step(
        half, obs_blocks.reshape((-1,) + obs_blocks.shape[2:]), table, xt, self_dots, norm,
        inner_perceptron_coeffs, outer_perceptron_coeffs, n_cells,
    )
    in_grad, out_grad = reduce_everywhere(half, keep, give, hidden_width)
    state_grid = revised_analysis.reshape(cell_rows, cell_cols, model_width)
    state_padded = extended(state_grid, (("lon", 1), ("lat", 0)), 1)
    analysis = (
        mix_local(state_padded, keep_rows, adjacent_channel_coeffs, 1)
        .astype(jnp.bfloat16)
        .reshape(hidden_member_fields.shape)
    )
    return (analysis, in_grad, out_grad)


def solution(mesh):
    in_specs = (
        P(("lat", "lon", "mem"), None, None),
        P(("lat", "lon", "mem")),
        P("mem", "lat", "lon", None),
        P("mem", "lat", "lon", None),
        P(),
        P(),
        P(),
        P(),
        P(),
    )
    out_specs = (P("mem", "lat", "lon", None), P(), P())

    return jax.shard_map(per_device, mesh=mesh, in_specs=in_specs, out_specs=out_specs, check_vma=False)
```
